32 devices in a mesh: dp: 8 (over z, x), row: 2 (over core), col: 2 (over y).
Axes of the slice: x: 2, y: 2, z: 4, core: 2. Of those that a mesh axis runs over, the one named last changes fastest.
Arguments:
- tokens: bfloat16 [12544, 512], P(('dp', 'row'), 'col'), may hold values from -6 to 6
- qkv_weight: bfloat16 [512, 3, 512], P('col', None, 'row'), may hold values from -0.25 to 0.25
- qkv_bias: float32 [2, 512], P(None, 'row'), may hold values from -3 to 3
- pos_table: float32 [169, 16], P(None, 'row'), may hold values from -4 to 304
- rel_index: int32 [49, 49], replicated, may hold values from 0 to 168
- region_ids: int32 [14, 14], replicated, may hold values from 0 to 2
- shifts: int32 [2], replicated, may hold values from 0 to 6
- proj_weight: bfloat16 [512, 512], P('row', 'col'), may hold values from -0.75 to 0.75
- proj_bias: float32 [512], P('col'), may hold values from -3 to 3
- layer_norm_scales: float32 [2, 512], P(None, 'col'), may hold values from 0.1 to 1.9
- layer_norm_biases: float32 [2, 512], P(None, 'col'), may hold values from -3 to 3
- fc1_weight: bfloat16 [512, 2048], P('col', 'row'), may hold values from -0.25 to 0.25
- fc1_bias: float32 [2048], P('row'), may hold values from -3 to 3
- fc2_weight: bfloat16 [2048, 512], P('row', 'col'), may hold values from -0.125 to 0.125
- fc2_bias: float32 [512], P('col'), may hold values from -3 to 3
- cotangent: bfloat16 [12544, 512], P(('dp', 'row'), 'col'), may hold values from -6 to 6
Outputs:
- out: bfloat16 [12544, 512], P(('dp', 'row'), 'col')
- grad_tokens: float32 [12544, 512], P(('dp', 'row'), 'col')
- grad_qkv: float32 [512, 3, 512], P('col', None, 'row')
- grad_qkv_bias: float32 [2, 512], P(None, 'row')
- grad_pos_table: float32 [169, 16], P(None, 'row')
- grad_proj: float32 [512, 512], P('row', 'col')
- grad_proj_bias: float32 [512], P('col')
- grad_gains: float32 [2, 512], P(None, 'col')
- grad_shifts: float32 [2, 512], P(None, 'col')
- grad_fc1: float32 [512, 2048], P('col', 'row')
- grad_fc1_bias: float32 [2048], P('row')
- grad_fc2: float32 [2048, 512], P('row', 'col')
- grad_fc2_bias: float32 [512], P('col')
The draws below stay inside these ranges and needn't reach their ends.
All inputs are finite; a program needn't handle non-finite values.
Results may differ from the reference program's by a relative error of at most 0.014.
Values may be sent and summed in bfloat16 or wider, within the bound.
No kernel may reach another device: no remote copies, remote signals or barrier semaphores. Data moves between devices by JAX's collectives and lax.ppermute only.
A program may use at most 128 MiB of HBM per device.

```python
import jax
import jax.numpy as jnp
from jax import lax

D = 512
HEADS = 16
HEAD_DIM = 32
FF = 2048
WIN = 7
SIDE = 14
IMG_GRP = 8
TABLE = 169
TOKENS = 12544


def draw_pos_table(key, part):
    base_key = jax.random.fold_in(jax.random.fold_in(key, 17), 0)
    return jnp.clip(jax.random.normal(base_key, (TABLE, HEADS), jnp.float32), -4.0, 4.0)


def place_ends(entries, rng, low, top_value):
    longest = entries.shape.index(max(entries.shape))
    spots = []
    for shift in (0, 1):
        where = [jax.random.randint(jax.random.fold_in(rng, axis), (), 0, length) for axis, length in enumerate(entries.shape)]
        where[longest] = (where[longest] + shift) % entries.shape[longest]
        spots.append(tuple(where))
    return entries.at[spots[0]].set(low).at[spots[1]].set(top_value)


def level_of(rng, extent, cuts, low, high):
    level = 1.0
    for position, blocks in cuts:
        draws = jax.random.uniform(jax.random.fold_in(jax.random.fold_in(rng, 6), position), (blocks,), jnp.float32, low / len(cuts), high / len(cuts))
        level = level * jnp.repeat(jnp.exp(draws), extent[position] // blocks).reshape((-1,) + (1,) * (len(extent) - 1 - position))
    return level


def noise(key, shape, width, most, cuts=(), dtype=jnp.bfloat16):
    level = level_of(key, shape, cuts, -0.22, 0.18) if cuts else 1.0
    values = jax.random.normal(key, shape, jnp.float32) * width * level
    return jnp.minimum(jnp.maximum(values, -most), most).astype(dtype)


def setup_inputs(seed: int = 0) -> dict:
    splits = jax.random.split(jax.random.key(seed), 17)
    tokens = noise(splits[0], (TOKENS, D), 1.0, 6.0, ((0, 16), (1, 2)))
    qkv_weight = noise(splits[1], (D, 3, D), D ** -0.5, 0.25, ((0, 2), (2, 2)))
    qkv_bias = noise(splits[2], (2, D), 0.5, 3.0, ((1, 2),), jnp.float32)
    pos_table = draw_pos_table(jax.random.fold_in(splits[16], 71), 0)
    rel_index = place_ends(jax.random.randint(splits[4], (WIN * WIN, WIN * WIN), 0, TABLE), jax.random.fold_in(splits[4], 1), 0, TABLE - 1).astype(jnp.int32)
    region_ids = place_ends(jax.random.randint(splits[5], (SIDE, SIDE), 0, 3), jax.random.fold_in(splits[5], 1), 0, 2).astype(jnp.int32)
    shifts = jax.random.randint(splits[6], (2,), 0, WIN).astype(jnp.int32)
    proj_weight = noise(splits[7], (D, D), (D // 8) ** -0.5, 0.75, ((0, 2), (1, 2)))
    proj_bias = noise(splits[8], (D,), 0.5, 3.0, ((0, 2),), jnp.float32)
    layer_norm_scales = jnp.clip(1.0 + 0.18 * jax.random.normal(splits[9], (2, D), jnp.float32), 0.1, 1.9)
    layer_norm_biases = noise(splits[10], (2, D), 0.5, 3.0, ((1, 2),), jnp.float32)
    fc1_weight = noise(splits[11], (D, FF), D ** -0.5, 0.25, ((0, 2), (1, 2)))
    fc1_bias = noise(splits[12], (FF,), 0.5, 3.0, ((0, 2),), jnp.float32)
    fc2_weight = noise(splits[13], (FF, D), FF ** -0.5, 0.125, ((0, 2), (1, 2)))
    fc2_bias = noise(splits[14], (D,), 0.5, 3.0, ((0, 2),), jnp.float32)
    cotangent = noise(splits[15], (TOKENS, D), 1.0, 6.0, ((0, 16), (1, 2)))
    return {"tokens": tokens, "qkv_weight": qkv_weight, "qkv_bias": qkv_bias, "pos_table": pos_table, "rel_index": rel_index, "region_ids": region_ids, "shifts": shifts, "proj_weight": proj_weight, "proj_bias": proj_bias, "layer_norm_scales": layer_norm_scales, "layer_norm_biases": layer_norm_biases, "fc1_weight": fc1_weight, "fc1_bias": fc1_bias, "fc2_weight": fc2_weight, "fc2_bias": fc2_bias, "cotangent": cotangent}


@jax.custom_vjp
def low(v):
    return lax.optimization_barrier(v.astype(jnp.bfloat16)).astype(jnp.float32)

@jax.custom_vjp
def low_back(v):
    return v

def low_keep(v):
    return (low(v), None)

def low_pass(kept, grad):
    return (grad,)

def back_keep(v):
    return (v, None)

def back_low(kept, grad):
    return (low(grad),)
low.defvjp(low_keep, low_pass)
low_back.defvjp(back_keep, back_low)
highest = lax.Precision.HIGHEST
epsilon = 1e-05
masked_value = -1000000000.0

def layer_norm(values, gain, offset):
    center = lax.optimization_barrier(jnp.mean(values, axis=-1, keepdims=True))
    centered = values - center
    variance = lax.optimization_barrier(jnp.mean(centered * centered, axis=-1, keepdims=True))
    return centered * lax.rsqrt(variance + epsilon) * gain + offset

def to_windows(values, shifts):
    channels = values.shape[-1]
    per_side = SIDE // WIN
    grid = values.reshape(-1, SIDE, SIDE, channels)
    grid = jnp.roll(grid, (-shifts[0], -shifts[1]), axis=(1, 2))
    grid = grid.reshape(-1, per_side, WIN, per_side, WIN, channels).transpose(0, 1, 3, 2, 4, 5)
    return grid.reshape(grid.shape[0], per_side * per_side, WIN * WIN, channels)

def from_windows(windows, shifts):
    channels = windows.shape[-1]
    per_side = SIDE // WIN
    grid = windows.reshape(-1, per_side, per_side, WIN, WIN, channels).transpose(0, 1, 3, 2, 4, 5)
    grid = jnp.roll(grid.reshape(-1, SIDE, SIDE, channels), (shifts[0], shifts[1]), axis=(1, 2))
    return grid.reshape(-1, channels)

def region_windows(region_ids):
    per_side = SIDE // WIN
    grid = region_ids.reshape(per_side, WIN, per_side, WIN).transpose(0, 2, 1, 3)
    return grid.reshape(per_side * per_side, WIN * WIN)

def layer(values, params, rel_index, region_ids, shifts):
    qkv_weight, qkv_bias, pos_table, proj_weight, proj_bias, layer_norm_scales, layer_norm_biases, fc1_weight, fc1_bias, fc2_weight, fc2_bias = params
    score_scale = HEAD_DIM ** (-0.5)
    normed = low(layer_norm(values, layer_norm_scales[0], layer_norm_biases[0]))
    projected = jnp.einsum('td,dke->tke', normed, qkv_weight, precision=highest)
    queries = low_back(low(projected[:, 0] + qkv_bias[0]))
    keys_tok = low_back(low(projected[:, 1]))
    values_tok = low_back(low(projected[:, 2] + qkv_bias[1]))

    def split_heads(tokens_in):
        windows = to_windows(tokens_in, shifts)
        return windows.reshape(windows.shape[:3] + (HEADS, HEAD_DIM))
    queries_win = split_heads(queries)
    keys_win = split_heads(keys_tok)
    values_win = split_heads(values_tok)
    pos_bias = jnp.transpose(pos_table[rel_index], (2, 0, 1))
    zone_ids = region_windows(region_ids)
    allowed = zone_ids[:, :, None] == zone_ids[:, None, :]
    raw_scores = jnp.einsum('nwqhd,nwkhd->nwhqk', queries_win, keys_win, precision=highest) * score_scale
    raw_scores = low_back(raw_scores + pos_bias[None, None])
    scores = jnp.where(allowed[None, :, None], raw_scores, masked_value)
    row_max = lax.optimization_barrier(jnp.max(scores, axis=-1, keepdims=True))
    exponent = jnp.exp(scores - row_max)
    attn_probs = low(exponent / lax.optimization_barrier(jnp.sum(exponent, axis=-1, keepdims=True)))
    attended = jnp.einsum('nwhqk,nwkhd->nwqhd', attn_probs, values_win, precision=highest)
    attended = low_back(low(attended))
    attended = from_windows(attended.reshape(attended.shape[:3] + (HEADS * HEAD_DIM,)), shifts)
    hidden = values + low_back(jnp.dot(attended, proj_weight, precision=highest) + proj_bias)
    second_normalized = low(layer_norm(hidden, layer_norm_scales[1], layer_norm_biases[1]))
    pre_act = low_back(jnp.dot(second_normalized, fc1_weight, precision=highest) + fc1_bias)
    activated = low(jax.nn.gelu(pre_act, approximate=False))
    branch_out = low_back(jnp.dot(activated, fc2_weight, precision=highest) + fc2_bias)
    return hidden + branch_out

def reference(tokens, qkv_weight, qkv_bias, pos_table, rel_index, region_ids, shifts, proj_weight, proj_bias, layer_norm_scales, layer_norm_biases, fc1_weight, fc1_bias, fc2_weight, fc2_bias, cotangent):
    per_block = IMG_GRP // 2 * SIDE * SIDE
    block_count = tokens.shape[0] // per_block

    def block_layer(block_rows, params):
        return layer(block_rows, params, rel_index, region_ids, shifts)
    checked = jax.checkpoint(block_layer)

    def forward(inputs, *params):
        stacked = inputs.reshape(block_count, per_block, inputs.shape[1])

        def scan_step(carry, block_rows):
            return (carry, checked(block_rows, params))
        carry, outputs = lax.scan(scan_step, None, stacked)
        return outputs.reshape(inputs.shape)
    floats = (qkv_weight.astype(jnp.float32), qkv_bias.astype(jnp.float32), pos_table.astype(jnp.float32), proj_weight.astype(jnp.float32), proj_bias.astype(jnp.float32), layer_norm_scales.astype(jnp.float32), layer_norm_biases.astype(jnp.float32), fc1_weight.astype(jnp.float32), fc1_bias.astype(jnp.float32), fc2_weight.astype(jnp.float32), fc2_bias.astype(jnp.float32))
    result, backward = jax.vjp(forward, tokens.astype(jnp.float32), *floats)
    grads = backward(cotangent.astype(jnp.float32))
    return (result.astype(jnp.bfloat16), grads[0], grads[1], grads[2], grads[3], grads[4], grads[5], grads[6], grads[7], grads[8], grads[9], grads[10], grads[11])
```

```python
import functools

import jax
import jax.numpy as jnp
from jax import lax
from jax.experimental import pallas as pl
from jax.experimental.pallas import tpu as pltpu
from jax.sharding import PartitionSpec as P

HEAD_DIM = 32
WIN = 7
SIDE = 14
CELLS = WIN * WIN
IMAGE = SIDE * SIDE
PAIR = 112
GROUP = 128 // HEAD_DIM

highest = lax.Precision.HIGHEST
epsilon = 1e-05
masked_value = -1000000000.0
score_scale = HEAD_DIM ** (-0.5)
f32 = jnp.float32
bf16 = jnp.bfloat16


def swap(values, axis, bit=0):
    size = lax.axis_size(axis)
    return lax.ppermute(values, axis, [(i, i ^ (1 << bit)) for i in range(size)])


def swap_row(values):
    return swap(values, "row")


def swap_col(values):
    return swap(values, "col")


def dot(a, b):
    return jnp.dot(a, b, preferred_element_type=f32)


def dot_nt(a, b):
    return lax.dot_general(a, b, (((1,), (1,)), ((), ())), preferred_element_type=f32)


def dot_tn(a, b):
    return lax.dot_general(a, b, (((0,), (0,)), ((), ())), preferred_element_type=f32)


def lane_group():
    return lax.broadcasted_iota(jnp.int32, (PAIR, 128), 1) // HEAD_DIM


def attend_kernel(q_ref, k_ref, v_ref, bias_ref, p_ref, o_ref):
    heads = bias_ref.shape[1]
    lanes = lane_group()
    for g in range(heads // GROUP):
        cols = slice(g * 128, (g + 1) * 128)
        q, k, v = q_ref[:, cols], k_ref[:, cols], v_ref[:, cols]
        total = jnp.zeros((PAIR, 128), f32)
        for j in range(GROUP):
            h = g * GROUP + j
            mine = lanes == j
            qh = jnp.where(mine, q, jnp.zeros_like(q))
            s = dot_nt(qh, k) * score_scale + bias_ref[0, h]
            e = jnp.exp(s - jnp.max(s, axis=-1, keepdims=True))
            p = (e / jnp.sum(e, axis=-1, keepdims=True)).astype(bf16)
            p_ref[0, h] = p
            total = jnp.where(mine, dot(p, v), total)
        o_ref[:, cols] = total.astype(bf16)


def attend_back_kernel(q_ref, k_ref, v_ref, p_ref, do_ref, dq_ref, dk_ref, dv_ref, ds_ref):
    heads = p_ref.shape[1]
    lanes = lane_group()

    @pl.when(pl.program_id(0) == 0)
    def _():
        ds_ref[...] = jnp.zeros_like(ds_ref)

    for g in range(heads // GROUP):
        cols = slice(g * 128, (g + 1) * 128)
        q, k, v, do = q_ref[:, cols], k_ref[:, cols], v_ref[:, cols], do_ref[:, cols]
        dq = jnp.zeros((PAIR, 128), f32)
        dk = jnp.zeros((PAIR, 128), f32)
        dv = jnp.zeros((PAIR, 128), f32)
        for j in range(GROUP):
            h = g * GROUP + j
            mine = lanes == j
            doh = jnp.where(mine, do, jnp.zeros_like(do))
            p = p_ref[0, h]
            pf = p.astype(f32)
            dp = dot_nt(doh, v)
            delta = jnp.sum(pf * dp, axis=-1, keepdims=True)
            dsf = pf * (dp - delta)
            ds = dsf.astype(bf16)
            ds_ref[h] += ds.astype(f32)
            dq = jnp.where(mine, dot(ds, k), dq)
            dk = jnp.where(mine, dot_tn(ds, q), dk)
            dv = jnp.where(mine, dot_tn(p, do), dv)
        dq_ref[:, cols] = (dq * score_scale).astype(bf16)
        dk_ref[:, cols] = (dk * score_scale).astype(bf16)
        dv_ref[:, cols] = dv.astype(bf16)


def attend(q, k, v, bias):
    rows, width = q.shape
    heads = width // HEAD_DIM
    pairs = rows // PAIR
    tile = pl.BlockSpec((PAIR, width), lambda i: (i, 0))
    return pl.pallas_call(
        attend_kernel,
        grid=(pairs,),
        in_specs=[tile, tile, tile, pl.BlockSpec((1, heads, PAIR, PAIR), lambda i: (i % 2, 0, 0, 0))],
        out_specs=[pl.BlockSpec((1, heads, PAIR, PAIR), lambda i: (i, 0, 0, 0)), tile],
        out_shape=[
            jax.ShapeDtypeStruct((pairs, heads, PAIR, PAIR), bf16),
            jax.ShapeDtypeStruct((rows, width), bf16),
        ],
        cost_estimate=pl.CostEstimate(flops=10**9, bytes_accessed=8 * 10**6, transcendentals=10**6),
        name="attend",
    )(q, k, v, bias)


def attend_back(q, k, v, probs, do):
    rows, width = q.shape
    heads = width // HEAD_DIM
    pairs = rows // PAIR
    tile = pl.BlockSpec((PAIR, width), lambda i: (i, 0))
    whole = pl.BlockSpec((heads, PAIR, PAIR), lambda i: (0, 0, 0))
    out = jax.ShapeDtypeStruct((rows, width), bf16)
    return pl.pallas_call(
        attend_back_kernel,
        grid=(pairs,),
        in_specs=[tile, tile, tile, pl.BlockSpec((1, heads, PAIR, PAIR), lambda i: (i, 0, 0, 0)), tile],
        out_specs=[tile, tile, tile, whole],
        out_shape=[out, out, out, jax.ShapeDtypeStruct((heads, PAIR, PAIR), f32)],
        cost_estimate=pl.CostEstimate(flops=2 * 10**9, bytes_accessed=8 * 10**6, transcendentals=0),
        name="attend_back",
    )(q, k, v, probs, do)


def norm(values):
    center = jnp.mean(values, axis=1, keepdims=True)
    centered = values - center
    scaling = lax.rsqrt(jnp.mean(centered * centered, axis=1, keepdims=True) + epsilon)
    return centered * scaling, scaling


def norm_back(grad, hat, scaling, gain):
    scaled = grad * gain
    first = jnp.mean(scaled, axis=1, keepdims=True)
    second = jnp.mean(scaled * hat, axis=1, keepdims=True)
    return (
        scaling * (scaled - first - hat * second),
        jnp.sum(grad * hat, axis=0),
        jnp.sum(grad, axis=0),
    )


def both_cols(vector):
    return jnp.concatenate([vector, swap_col(vector)], axis=-1)


def both_rows(vector):
    return jnp.concatenate([vector, swap_row(vector)], axis=-1)


def gather_weight(weight, col_dim, row_dim):
    mine = jnp.concatenate([weight, swap_row(weight)], axis=row_dim)
    other = swap_col(weight)
    other = jnp.concatenate([other, swap_row(other)], axis=row_dim)
    return jnp.concatenate([mine, other], axis=col_dim)


def reduce_dp(block):
    size = lax.axis_size("dp")
    bits = size.bit_length() - 1
    me = lax.axis_index("dp")
    for bit in range(bits):
        half = block.shape[0] // 2
        side = (me >> bit) & 1
        keep = lax.dynamic_slice_in_dim(block, side * half, half, 0)
        send = lax.dynamic_slice_in_dim(block, (1 - side) * half, half, 0)
        block = keep + swap(send, "dp", bit)
    for bit in reversed(range(bits)):
        side = (me >> bit) & 1
        other = swap(block, "dp", bit)
        block = jnp.where(
            side == 0,
            jnp.concatenate([block, other], axis=0),
            jnp.concatenate([other, block], axis=0),
        )
    return block


def reduce_weight(grad, col_dim, row_dim):
    half = grad.shape[row_dim] // 2
    keep = lax.slice_in_dim(grad, 0, half, axis=row_dim)
    send = lax.slice_in_dim(grad, half, 2 * half, axis=row_dim)
    grad = keep + swap_row(send)
    half = grad.shape[col_dim] // 2
    keep = lax.slice_in_dim(grad, 0, half, axis=col_dim)
    send = lax.slice_in_dim(grad, half, 2 * half, axis=col_dim)
    grad = keep + swap_col(send)
    shape = grad.shape
    return reduce_dp(grad.reshape(-1, shape[-1])).reshape(shape).astype(f32)


def shards(
    tokens,
    qkv_weight,
    qkv_bias,
    pos_table,
    rel_index,
    region_ids,
    shifts,
    proj_weight,
    proj_bias,
    layer_norm_scales,
    layer_norm_biases,
    fc1_weight,
    fc1_bias,
    fc2_weight,
    fc2_bias,
    cotangent,
):
    col = lax.axis_index("col")
    block_rows = tokens.shape[0]
    rows = block_rows // 2
    images = rows // IMAGE

    def exchange(values):
        keep = lax.dynamic_slice_in_dim(values, col * rows, rows, 0)
        send = lax.dynamic_slice_in_dim(values, (1 - col) * rows, rows, 0)
        return jnp.concatenate([keep, swap_col(send)], axis=1)

    def give_back(values):
        half = values.shape[1] // 2
        keep, send = values[:, :half], values[:, half:]
        other = swap_col(send.astype(bf16)).astype(values.dtype)
        return jnp.where(
            col == 0,
            jnp.concatenate([keep, other], axis=0),
            jnp.concatenate([other, keep], axis=0),
        )

    x_tok = exchange(tokens)
    wqkv = gather_weight(qkv_weight, 0, 2)
    wqkv = wqkv.reshape(wqkv.shape[0], -1)
    wproj = gather_weight(proj_weight, 1, 0)
    wfc1 = gather_weight(fc1_weight, 0, 1)
    z_tok = exchange(cotangent)
    wfc2 = gather_weight(fc2_weight, 1, 0)
    col_vectors = both_cols(
        jnp.stack(
            [
                layer_norm_scales[0],
                layer_norm_scales[1],
                layer_norm_biases[0],
                layer_norm_biases[1],
                proj_bias,
                fc2_bias,
            ]
        )
    )
    gain_one, gain_two, shift_one, shift_two, bias_proj, bias_fc2 = col_vectors
    bias_fc1 = both_rows(fc1_bias)
    bias_qkv = both_rows(qkv_bias)
    table = both_rows(pos_table)
    heads = table.shape[1]

    place = jnp.arange(2 * PAIR, dtype=jnp.int32)
    pair, inside = place // PAIR, place % PAIR
    window = 2 * pair + inside // CELLS
    spot = inside % CELLS
    cell_i = (window // 2) * WIN + spot // WIN
    cell_j = (window % 2) * WIN + spot % WIN
    token = ((cell_i + shifts[0]) % SIDE) * SIDE + (cell_j + shifts[1]) % SIDE
    token = jnp.where(inside < 2 * CELLS, token, -1)
    order = (token[:, None] == jnp.arange(IMAGE, dtype=jnp.int32)[None, :]).astype(bf16)

    def to_rows(values):
        stacked = values.reshape(images, IMAGE, values.shape[1])
        return jnp.einsum("ra,nad->nrd", order, stacked, preferred_element_type=f32).reshape(
            -1, values.shape[1]
        )

    def to_tokens(values):
        stacked = values.reshape(images, 2 * PAIR, values.shape[1])
        return jnp.einsum("ra,nrd->nad", order, stacked, preferred_element_type=f32).reshape(
            -1, values.shape[1]
        )

    lookup = (rel_index.reshape(-1)[:, None] == jnp.arange(table.shape[0])[None, :]).astype(f32)
    pos = jnp.dot(lookup, table, precision=highest).T.reshape(heads, CELLS, CELLS)
    per_side = SIDE // WIN
    zones = region_ids.reshape(per_side, WIN, per_side, WIN).transpose(0, 2, 1, 3)
    zones = zones.reshape(per_side * per_side, CELLS)
    allowed = zones[:, :, None] == zones[:, None, :]
    biased = jnp.where(allowed[:, None], pos[None], masked_value)
    spare = PAIR - 2 * CELLS

    def corner(values, low):
        high = PAIR - low - CELLS
        return jnp.pad(
            values, ((0, 0), (0, 0), (low, high), (low, high)), constant_values=masked_value
        )

    bias = jnp.maximum(corner(biased[0::2], 0), corner(biased[1::2], CELLS))

    x = to_rows(x_tok)
    hat_one, inv_one = norm(x)
    a1 = (hat_one * gain_one + shift_one).astype(bf16)
    projected = dot(a1, wqkv).reshape(a1.shape[0], 3, -1)
    q = (projected[:, 0] + bias_qkv[0]).astype(bf16)
    k = projected[:, 1].astype(bf16)
    v = (projected[:, 2] + bias_qkv[1]).astype(bf16)
    probs, o = attend(q, k, v, bias)
    h1 = x + dot(o, wproj) + bias_proj
    hat_two, inv_two = norm(h1)
    a2 = (hat_two * gain_two + shift_two).astype(bf16)
    pre = dot(a2, wfc1) + bias_fc1
    cdf = 0.5 * (1.0 + lax.erf(pre * (0.5**0.5)))
    m = (pre * cdf).astype(bf16)
    slope = cdf + pre * (jnp.exp(-0.5 * pre * pre) * 0.3989422804014327)
    out_rows = (h1 + dot(m, wfc2) + bias_fc2).astype(bf16)
    out = give_back(to_tokens(out_rows).astype(bf16))

    dz_low = to_rows(z_tok).astype(bf16)
    dz = dz_low.astype(f32)
    fc2_grad = reduce_weight(dot_tn(m, dz_low).astype(bf16), 1, 0)
    df = (dot_nt(dz_low, wfc2) * slope).astype(bf16)
    fc1_grad = reduce_weight(dot_tn(a2, df).astype(bf16), 0, 1)
    du, gain_two_part, shift_two_part = norm_back(dot_nt(df, wfc1), hat_two, inv_two, gain_two)
    dh1 = dz + du
    dy = dh1.astype(bf16)
    proj_grad = reduce_weight(dot_tn(o, dy).astype(bf16), 1, 0)
    do = dot_nt(dy, wproj).astype(bf16)
    dq, dk, dv, ds = attend_back(q, k, v, probs, do)
    dqkv = jnp.concatenate([dq, dk, dv], axis=1)
    qkv_part = dot_tn(a1, dqkv).astype(bf16).reshape(wqkv.shape[0], 3, -1)
    qkv_grad = reduce_weight(qkv_part, 0, 2)
    du, gain_one_part, shift_one_part = norm_back(dot_nt(dqkv, wqkv), hat_one, inv_one, gain_one)
    grad_rows = (dh1 + du).astype(bf16)
    grad_input = give_back(to_tokens(grad_rows))

    ds_sum = ds[:, :CELLS, :CELLS] + ds[:, CELLS : 2 * CELLS, CELLS : 2 * CELLS]
    table_part = lax.dot_general(
        lookup, ds_sum.reshape(heads, -1), (((0,), (1,)), ((), ())), precision=highest
    )

    def total(v):
        return jnp.sum(v, axis=0, dtype=f32)

    row_parts = [
        jnp.stack([total(dq), total(dv)]),
        table_part,
        total(df)[None],
    ]
    col_parts = jnp.stack(
        [gain_one_part, gain_two_part, shift_one_part, shift_two_part, total(dy), total(dz)]
    )
    row_halves = [jnp.split(p, 2, axis=1) for p in row_parts]
    col_halves = jnp.split(col_parts, 2, axis=1)
    keep_r = jnp.concatenate([h[0].reshape(-1) for h in row_halves])
    send_r = jnp.concatenate([h[1].reshape(-1) for h in row_halves])
    both_c = jnp.concatenate([h.reshape(-1) for h in col_halves])
    n_r, n_c = keep_r.shape[0], both_c.shape[0] // 2
    got = swap_row(jnp.concatenate([send_r, both_c]))
    keep_r = keep_r + got[:n_r]
    both_c = both_c + got[n_r:]
    got = swap_col(jnp.concatenate([keep_r, both_c[n_c:]]))
    small = jnp.concatenate([keep_r, both_c[:n_c]]) + got
    size = lax.axis_size("dp")
    for bit in range(size.bit_length() - 1):
        small = small + swap(small, "dp", bit)
    r_shapes = [h[0].shape for h in row_halves]
    pieces, at = [], 0
    for shape in r_shapes:
        count = shape[0] * shape[1]
        pieces.append(small[at : at + count].reshape(shape))
        at += count
    qkv_bias_grad, table_grad, fc1_bias_grad = pieces
    cols = small[n_r:].reshape(col_halves[0].shape)
    return (
        out,
        grad_input.astype(f32),
        qkv_grad,
        qkv_bias_grad,
        table_grad,
        proj_grad,
        cols[4],
        cols[0:2],
        cols[2:4],
        fc1_grad,
        fc1_bias_grad[0],
        fc2_grad,
        cols[5],
    )


def solution(mesh):
    return jax.shard_map(
        shards,
        mesh=mesh,
        in_specs=(
            P(("dp", "row"), "col"),
            P("col", None, "row"),
            P(None, "row"),
            P(None, "row"),
            P(),
            P(),
            P(),
            P("row", "col"),
            P("col"),
            P(None, "col"),
            P(None, "col"),
            P("col", "row"),
            P("row"),
            P("row", "col"),
            P("col"),
            P(("dp", "row"), "col"),
        ),
        out_specs=(
            P(("dp", "row"), "col"),
            P(("dp", "row"), "col"),
            P("col", None, "row"),
            P(None, "row"),
            P(None, "row"),
            P("row", "col"),
            P("col"),
            P(None, "col"),
            P(None, "col"),
            P("col", "row"),
            P("row"),
            P("row", "col"),
            P("col"),
        ),
        check_vma=False,
    )
```

```python
import functools

import jax
import jax.numpy as jnp
from jax import lax
from jax.experimental import pallas as pl
from jax.experimental.pallas import tpu as pltpu
from jax.sharding import PartitionSpec as P

HEAD_DIM = 32
WIN = 7
SIDE = 14
CELLS = WIN * WIN
IMAGE = SIDE * SIDE
PAIR = 112
GROUP = 128 // HEAD_DIM

highest = lax.Precision.HIGHEST
epsilon = 1e-05
masked_value = -1000000000.0
score_scale = HEAD_DIM ** (-0.5)
f32 = jnp.float32
bf16 = jnp.bfloat16


def swap(values, axis, bit=0):
    size = lax.axis_size(axis)
    return lax.ppermute(values, axis, [(i, i ^ (1 << bit)) for i in range(size)])


def swap_row(values):
    return swap(values, "row")


def swap_col(values):
    return swap(values, "col")


def dot(a, b):
    return jnp.dot(a, b, preferred_element_type=f32)


def dot_nt(a, b):
    return lax.dot_general(a, b, (((1,), (1,)), ((), ())), preferred_element_type=f32)


def dot_tn(a, b):
    return lax.dot_general(a, b, (((0,), (0,)), ((), ())), preferred_element_type=f32)


def lane_group():
    return lax.broadcasted_iota(jnp.int32, (PAIR, 128), 1) // HEAD_DIM


def fill_lanes(rows):
    return jnp.concatenate([rows, jnp.zeros((128 - PAIR, 128), rows.dtype)], axis=0)


def attend_kernel(q_ref, k_ref, v_ref, bias_ref, p_ref, o_ref):
    lanes = lane_group()
    for g in range(bias_ref.shape[1] // GROUP):
        cols = slice(g * 128, (g + 1) * 128)
        q = fill_lanes(q_ref[:, cols])
        k = k_ref[:, cols]
        v_t = v_ref[:, cols].T
        parts = []
        for j in range(GROUP):
            h = g * GROUP + j
            kh = jnp.where(lanes == j, k, jnp.zeros_like(k))
            s = dot_nt(kh, q) * score_scale + bias_ref[0, h]
            e = jnp.exp(s - jnp.max(s, axis=0, keepdims=True))
            p = (e * (1.0 / jnp.sum(e, axis=0, keepdims=True))).astype(bf16)
            p_ref[0, h] = p
            parts.append(dot(v_t[j * HEAD_DIM : (j + 1) * HEAD_DIM], p))
        o_ref[:, cols] = jnp.concatenate(parts, axis=0).T[:PAIR].astype(bf16)


def attend_back_kernel(q_ref, k_ref, v_ref, p_ref, do_ref, dq_ref, dk_ref, dv_ref, ds_ref):
    lanes = lane_group()

    @pl.when(pl.program_id(0) == 0)
    def _():
        ds_ref[...] = jnp.zeros_like(ds_ref)

    for g in range(p_ref.shape[1] // GROUP):
        cols = slice(g * 128, (g + 1) * 128)
        q, k, v, do = q_ref[:, cols], k_ref[:, cols], v_ref[:, cols], do_ref[:, cols]
        zero = jnp.zeros_like(q)
        do_full = fill_lanes(do)
        k_t = k.T
        dq, ds_all, p_all, q_all, do_all = [], [], [], [], []
        for j in range(GROUP):
            h = g * GROUP + j
            mine = lanes == j
            p = p_ref[0, h]
            pf = p.astype(f32)
            dp = dot_nt(jnp.where(mine, v, zero), do_full)
            ds = pf * (dp - jnp.sum(pf * dp, axis=0, keepdims=True))
            ds = ds.astype(bf16)
            ds_ref[h] += ds.astype(f32)
            dq.append(dot(k_t[j * HEAD_DIM : (j + 1) * HEAD_DIM], ds))
            ds_all.append(ds)
            p_all.append(p)
            q_all.append(fill_lanes(jnp.where(mine, q, zero)))
            do_all.append(fill_lanes(jnp.where(mine, do, zero)))
        dk = dot(jnp.concatenate(ds_all, axis=1), jnp.concatenate(q_all, axis=0))
        dv = dot(jnp.concatenate(p_all, axis=1), jnp.concatenate(do_all, axis=0))
        dq = jnp.concatenate(dq, axis=0).T[:PAIR]
        dq_ref[:, cols] = (dq * score_scale).astype(bf16)
        dk_ref[:, cols] = (dk * score_scale).astype(bf16)
        dv_ref[:, cols] = dv.astype(bf16)


def attend(q, k, v, bias):
    rows, width = q.shape
    heads = width // HEAD_DIM
    pairs = rows // PAIR
    tile = pl.BlockSpec((PAIR, width), lambda i: (i, 0))
    return pl.pallas_call(
        attend_kernel,
        grid=(pairs,),
        in_specs=[tile, tile, tile, pl.BlockSpec((1, heads, PAIR, 128), lambda i: (i % 2, 0, 0, 0))],
        out_specs=[pl.BlockSpec((1, heads, PAIR, 128), lambda i: (i, 0, 0, 0)), tile],
        out_shape=[
            jax.ShapeDtypeStruct((pairs, heads, PAIR, 128), bf16),
            jax.ShapeDtypeStruct((rows, width), bf16),
        ],
        cost_estimate=pl.CostEstimate(flops=10**9, bytes_accessed=8 * 10**6, transcendentals=10**6),
        name="attend",
    )(q, k, v, bias)


def attend_back(q, k, v, probs, do):
    rows, width = q.shape
    heads = width // HEAD_DIM
    pairs = rows // PAIR
    tile = pl.BlockSpec((PAIR, width), lambda i: (i, 0))
    whole = pl.BlockSpec((heads, PAIR, 128), lambda i: (0, 0, 0))
    out = jax.ShapeDtypeStruct((rows, width), bf16)
    return pl.pallas_call(
        attend_back_kernel,
        grid=(pairs,),
        in_specs=[tile, tile, tile, pl.BlockSpec((1, heads, PAIR, 128), lambda i: (i, 0, 0, 0)), tile],
        out_specs=[tile, tile, tile, whole],
        out_shape=[out, out, out, jax.ShapeDtypeStruct((heads, PAIR, 128), f32)],
        cost_estimate=pl.CostEstimate(flops=2 * 10**9, bytes_accessed=8 * 10**6, transcendentals=0),
        name="attend_back",
    )(q, k, v, probs, do)


def chunked(rows, body):
    @pl.loop(0, rows // PAIR)
    def _(i):
        body(pl.ds(pl.multiple_of(i * PAIR, PAIR), PAIR))


def standardize(values):
    center = jnp.mean(values, axis=1, keepdims=True)
    centered = values - center
    scaling = lax.rsqrt(jnp.mean(centered * centered, axis=1, keepdims=True) + epsilon)
    return centered * scaling, scaling


def standardize_back(grad, hat, scaling, gain):
    scaled = grad * gain
    first = jnp.mean(scaled, axis=1, keepdims=True)
    second = jnp.mean(scaled * hat, axis=1, keepdims=True)
    return scaling * (scaled - first - hat * second)


def add_sum(ref, row, values):
    ref[row : row + 1, :] += jnp.sum(values, axis=0, keepdims=True)


GAIN1, GAIN2, SHIFT1, SHIFT2, BIAS_PROJ, BIAS_FC2 = range(6)
HALF = 256


def enter_kernel(own_ref, other_ref, order_ref, vec_ref, x_ref, a_ref):
    images = own_ref.shape[0] // IMAGE
    for n in range(images):
        rows = slice(n * IMAGE, (n + 1) * IMAGE)
        tok = jnp.concatenate([own_ref[rows], other_ref[rows]], axis=1)
        x = dot(order_ref[...], tok)
        hat, _ = standardize(x)
        a = hat * vec_ref[GAIN1 : GAIN1 + 1] + vec_ref[SHIFT1 : SHIFT1 + 1]
        out = slice(n * 2 * PAIR, (n + 1) * 2 * PAIR)
        x_ref[out] = x.astype(bf16)
        a_ref[out] = a.astype(bf16)


def qkv_kernel(a_ref, w0, w1, w2, w3, bias_ref, q_ref, k_ref, v_ref):
    for side, (top, low) in enumerate(((w0, w2), (w1, w3))):
        cols = slice(side * HALF, (side + 1) * HALF)
        for j, ref in enumerate((q_ref, k_ref, v_ref)):
            at = slice(j * HALF, (j + 1) * HALF)
            y = dot(a_ref[:, :HALF], top[:, at]) + dot(a_ref[:, HALF:], low[:, at])
            if j != 1:
                y = y + bias_ref[j // 2 : j // 2 + 1, cols]
            ref[:, cols] = y.astype(bf16)


def proj_kernel(x_ref, o_ref, w0, w1, w2, w3, vec_ref, h_ref, a_ref):
    def body(rows):
        o0, o1 = o_ref[rows, :HALF], o_ref[rows, HALF:]
        y = jnp.concatenate(
            [dot(o0, w0[...]) + dot(o1, w1[...]), dot(o0, w2[...]) + dot(o1, w3[...])], axis=1
        )
        h = x_ref[rows].astype(f32) + y + vec_ref[BIAS_PROJ : BIAS_PROJ + 1]
        hat, _ = standardize(h)
        h_ref[rows] = h
        a_ref[rows] = (
            hat * vec_ref[GAIN2 : GAIN2 + 1] + vec_ref[SHIFT2 : SHIFT2 + 1]
        ).astype(bf16)

    chunked(x_ref.shape[0], body)


def mlp_kernel(
    a_ref,
    dz_ref,
    h_ref,
    u0,
    u1,
    u2,
    u3,
    w0,
    w1,
    w2,
    w3,
    bias_ref,
    vec_ref,
    out_ref,
    da_ref,
    send2_ref,
    keep2_ref,
    send1_ref,
    keep1_ref,
    bsum_ref,
    acc_ref,
    at_ref,
):
    hidden = u0.shape[1]
    at_ref[...] = a_ref[...].T
    acc_ref[...] = h_ref[...] + vec_ref[BIAS_FC2 : BIAS_FC2 + 1]
    da_ref[...] = jnp.zeros_like(da_ref)
    for side, (up0, up1, down0, down1, grad2, grad1) in enumerate(
        ((u1, u3, w1, w3, send2_ref, send1_ref), (u0, u2, w0, w2, keep2_ref, keep1_ref))
    ):
        base = (1 - side) * hidden

        @pl.loop(0, hidden // HALF)
        def _(t, up0=up0, up1=up1, down0=down0, down1=down1, grad2=grad2, grad1=grad1, base=base):
            tile = pl.ds(pl.multiple_of(t * HALF, HALF), HALF)
            where = pl.ds(pl.multiple_of(base + t * HALF, HALF), HALF)
            p0, p1 = up0[:, tile], up1[:, tile]
            d0, d1 = down0[tile], down1[tile]
            z0, z1 = dz_ref[:, :HALF], dz_ref[:, HALF:]
            f = dot(a_ref[:, :HALF], p0) + dot(a_ref[:, HALF:], p1) + bias_ref[:, where]
            dm = dot_nt(z0, d0) + dot_nt(z1, d1)
            cdf = 0.5 * (1.0 + lax.erf(f * (0.5**0.5)))
            m = (f * cdf).astype(bf16)
            slope = cdf + f * (jnp.exp(-0.5 * f * f) * 0.3989422804014327)
            df = (dm * slope).astype(bf16)
            bsum_ref[:, where] = jnp.sum(df.astype(f32), axis=0, keepdims=True)
            acc_ref[:, :HALF] += dot(m, d0)
            acc_ref[:, HALF:] += dot(m, d1)
            da_ref[:, :HALF] += dot_nt(df, p0)
            da_ref[:, HALF:] += dot_nt(df, p1)
            mt = m.T
            grad2[0, tile] = dot(mt, z0).astype(bf16)
            grad2[1, tile] = dot(mt, z1).astype(bf16)
            grad1[0, :, tile] = dot(at_ref[:HALF], df).astype(bf16)
            grad1[1, :, tile] = dot(at_ref[HALF:], df).astype(bf16)

    out_ref[...] = acc_ref[...].astype(bf16)


def mid_kernel(
    da_ref, h_ref, dz_ref, o_ref, w0, w1, w2, w3, vec_ref, dh_ref, do_ref, send_ref, keep_ref, sum_ref, dy_ref
):
    sum_ref[...] = jnp.zeros_like(sum_ref)

    def body(rows):
        hat, scaling = standardize(h_ref[rows])
        da = da_ref[rows]
        dz = dz_ref[rows].astype(f32)
        du = standardize_back(da, hat, scaling, vec_ref[GAIN2 : GAIN2 + 1])
        dh = dz + du
        dh_ref[rows] = dh
        dy = dh.astype(bf16)
        dy_ref[rows] = dy
        y0, y1 = dy[:, :HALF], dy[:, HALF:]
        do_ref[rows] = jnp.concatenate(
            [dot_nt(y0, w0[...]) + dot_nt(y1, w2[...]), dot_nt(y0, w1[...]) + dot_nt(y1, w3[...])],
            axis=1,
        ).astype(bf16)
        add_sum(sum_ref, 0, da * hat)
        add_sum(sum_ref, 1, da)
        add_sum(sum_ref, 2, dy.astype(f32))
        add_sum(sum_ref, 3, dz)

    chunked(h_ref.shape[0], body)
    ot = o_ref[...].T
    for side, ref in enumerate((keep_ref, send_ref)):
        for c in range(2):
            ref[c] = dot(
                ot[side * HALF : (side + 1) * HALF], dy_ref[:, c * HALF : (c + 1) * HALF]
            ).astype(bf16)


def qkv_grad_kernel(a_ref, dq_ref, dk_ref, dv_ref, send_ref, keep_ref, sum_ref):
    at = a_ref[...].T
    for side, ref in enumerate((keep_ref, send_ref)):
        cols = slice(side * HALF, (side + 1) * HALF)
        for j, d_ref in enumerate((dq_ref, dk_ref, dv_ref)):
            d = d_ref[:, cols]
            for c in range(2):
                ref[c, :, j * HALF : (j + 1) * HALF] = dot(at[c * HALF : (c + 1) * HALF], d).astype(
                    bf16
                )
            if j != 1:
                sum_ref[j // 2 : j // 2 + 1, cols] = jnp.sum(d.astype(f32), axis=0, keepdims=True)


def leave_kernel(
    dq_ref, dk_ref, dv_ref, dh_ref, x_ref, w0, w1, w2, w3, vec_ref, order_ref, own_ref, other_ref, sum_ref, g_ref
):
    sum_ref[...] = jnp.zeros_like(sum_ref)

    def body(rows):
        da = []
        for top, low in ((w0, w1), (w2, w3)):
            part = None
            for j, ref in enumerate((dq_ref, dk_ref, dv_ref)):
                at = slice(j * HALF, (j + 1) * HALF)
                y = dot_nt(ref[rows, :HALF], top[:, at]) + dot_nt(ref[rows, HALF:], low[:, at])
                part = y if part is None else part + y
            da.append(part)
        da = jnp.concatenate(da, axis=1)
        hat, scaling = standardize(x_ref[rows].astype(f32))
        du = standardize_back(da, hat, scaling, vec_ref[GAIN1 : GAIN1 + 1])
        g_ref[rows] = (dh_ref[rows] + du).astype(bf16)
        add_sum(sum_ref, 0, da * hat)
        add_sum(sum_ref, 1, da)

    chunked(x_ref.shape[0], body)
    restore(g_ref, order_ref, own_ref, other_ref)


def restore(rows_ref, order_ref, own_ref, other_ref):
    images = own_ref.shape[0] // IMAGE
    for n in range(images):
        g = dot_tn(order_ref[...], rows_ref[n * 2 * PAIR : (n + 1) * 2 * PAIR])
        out = slice(n * IMAGE, (n + 1) * IMAGE)
        own_ref[out] = g[:, :HALF].astype(bf16)
        other_ref[out] = g[:, HALF:].astype(bf16)


def restore_kernel(rows_ref, order_ref, own_ref, other_ref):
    restore(rows_ref, order_ref, own_ref, other_ref)


def arrange_kernel(tok_ref, order_ref, out_ref):
    images = tok_ref.shape[0] // IMAGE
    for n in range(images):
        out_ref[n * 2 * PAIR : (n + 1) * 2 * PAIR] = dot(
            order_ref[...], tok_ref[n * IMAGE : (n + 1) * IMAGE]
        ).astype(bf16)


def call(kernel, name, args, outs, scratch=(), flops=10**9):
    space = pl.BlockSpec(memory_space=pltpu.VMEM)
    with jax.named_scope(name):
        return pl.pallas_call(
            kernel,
            in_specs=[space] * len(args),
            out_specs=[space] * len(outs),
            out_shape=[jax.ShapeDtypeStruct(shape, dtype) for shape, dtype in outs],
            scratch_shapes=[pltpu.VMEM(shape, dtype) for shape, dtype in scratch],
            cost_estimate=pl.CostEstimate(flops=flops, bytes_accessed=4 * 10**6, transcendentals=0),
            name=name,
        )(*args)


def both_cols(vector):
    return jnp.concatenate([vector, swap_col(vector)], axis=-1)


def both_rows(vector):
    return jnp.concatenate([vector, swap_row(vector)], axis=-1)


def gather_weight(weight, name):
    with jax.named_scope(name + "_row"):
        mine = swap_row(weight)
    with jax.named_scope(name + "_col"):
        other = swap_col(weight)
    with jax.named_scope(name + "_far"):
        return weight, mine, other, swap_row(other)


def reduce_dp(block, name):
    size = lax.axis_size("dp")
    bits = size.bit_length() - 1
    me = lax.axis_index("dp")
    for bit in range(bits):
        half = block.shape[0] // 2
        side = (me >> bit) & 1
        keep = lax.dynamic_slice_in_dim(block, side * half, half, 0)
        send = lax.dynamic_slice_in_dim(block, (1 - side) * half, half, 0)
        with jax.named_scope(f"{name}_h{bit}"):
            got = swap(send, "dp", bit)
        block = keep + got
    for bit in reversed(range(bits)):
        side = (me >> bit) & 1
        with jax.named_scope(f"{name}_d{bit}"):
            other = swap(block, "dp", bit)
        block = jnp.where(
            side == 0,
            jnp.concatenate([block, other], axis=0),
            jnp.concatenate([other, block], axis=0),
        )
    return block


def reduce_weight(send, keep, name):
    with jax.named_scope(name + "_r"):
        got = swap_row(send)
    pair = keep[1] + got[1]
    with jax.named_scope(name + "_c"):
        other = swap_col(pair)
    block = keep[0] + got[0] + other
    return reduce_dp(block, name).astype(f32)


def shards(
    tokens,
    qkv_weight,
    qkv_bias,
    pos_table,
    rel_index,
    region_ids,
    shifts,
    proj_weight,
    proj_bias,
    layer_norm_scales,
    layer_norm_biases,
    fc1_weight,
    fc1_bias,
    fc2_weight,
    fc2_bias,
    cotangent,
):
    col = lax.axis_index("col")
    block_rows = tokens.shape[0]
    rows = block_rows // 2

    def exchange(values, name):
        keep = lax.dynamic_slice_in_dim(values, col * rows, rows, 0)
        send = lax.dynamic_slice_in_dim(values, (1 - col) * rows, rows, 0)
        with jax.named_scope(name):
            return keep, swap_col(send)

    def give_back(keep, send, dtype, name):
        with jax.named_scope(name):
            other = swap_col(send)
        keep, other = keep.astype(dtype), other.astype(dtype)
        return jnp.where(
            col == 0,
            jnp.concatenate([keep, other], axis=0),
            jnp.concatenate([other, keep], axis=0),
        )

    x_own, x_other = exchange(tokens, "x")
    wqkv = gather_weight(qkv_weight.reshape(qkv_weight.shape[0], -1), "wqkv")
    wproj = gather_weight(proj_weight, "wproj")
    wfc1 = gather_weight(fc1_weight, "wfc1")
    z_own, z_other = exchange(cotangent, "z")
    wfc2 = gather_weight(fc2_weight, "wfc2")
    col_vectors = both_cols(
        jnp.stack(
            [
                layer_norm_scales[0],
                layer_norm_scales[1],
                layer_norm_biases[0],
                layer_norm_biases[1],
                proj_bias,
                fc2_bias,
            ]
        )
    )
    bias_fc1 = both_rows(fc1_bias)
    bias_qkv = both_rows(qkv_bias)
    table = both_rows(pos_table)
    heads = table.shape[1]

    place = jnp.arange(2 * PAIR, dtype=jnp.int32)
    pair, inside = place // PAIR, place % PAIR
    window = 2 * pair + inside // CELLS
    spot = inside % CELLS
    cell_i = (window // 2) * WIN + spot // WIN
    cell_j = (window % 2) * WIN + spot % WIN
    token = ((cell_i + shifts[0]) % SIDE) * SIDE + (cell_j + shifts[1]) % SIDE
    token = jnp.where(inside < 2 * CELLS, token, -1)
    order = (token[:, None] == jnp.arange(IMAGE, dtype=jnp.int32)[None, :]).astype(bf16)

    lookup = (rel_index.T.reshape(-1)[:, None] == jnp.arange(table.shape[0])[None, :]).astype(f32)
    pos = jnp.dot(lookup, table, precision=highest).T.reshape(heads, CELLS, CELLS)
    per_side = SIDE // WIN
    zones = region_ids.reshape(per_side, WIN, per_side, WIN).transpose(0, 2, 1, 3)
    zones = zones.reshape(per_side * per_side, CELLS)
    allowed = zones[:, :, None] == zones[:, None, :]
    biased = jnp.where(allowed[:, None], pos[None], masked_value)

    def corner(values, low):
        high = PAIR - low - CELLS
        return jnp.pad(
            values, ((0, 0), (0, 0), (low, high), (low, high + 128 - PAIR)), constant_values=masked_value
        )

    bias = jnp.maximum(corner(biased[0::2], 0), corner(biased[1::2], CELLS))

    count = rows // IMAGE * 2 * PAIR
    width = 2 * tokens.shape[1]
    wide = (count, width)
    x, a1 = call(enter_kernel, "k_enter", (x_own, x_other, order, col_vectors), [(wide, bf16)] * 2)
    q, k, v = call(qkv_kernel, "k_qkv", (a1, *wqkv, bias_qkv), [(wide, bf16)] * 3)
    with jax.named_scope("k_attend"):
        probs, o = attend(q, k, v, bias)
    h1, a2 = call(
        proj_kernel, "k_proj", (x, o, *wproj, col_vectors), [(wide, f32), (wide, bf16)]
    )
    (dz,) = call(
        arrange_kernel,
        "k_arrange",
        (jnp.concatenate([z_own, z_other], axis=1), order),
        [(wide, bf16)],
    )
    block2 = ((2, *fc2_weight.shape), bf16)
    block1 = ((2, *fc1_weight.shape), bf16)
    out_rows, da2, send2, keep2, send1, keep1, df_sum = call(
        mlp_kernel,
        "k_mlp",
        (a2, dz, h1, *wfc1, *wfc2, bias_fc1[None], col_vectors),
        [
            (wide, bf16),
            (wide, f32),
            block2,
            block2,
            block1,
            block1,
            ((1, bias_fc1.shape[0]), f32),
        ],
        scratch=[(wide, f32), (wide[::-1], bf16)],
        flops=3 * 10**9,
    )
    fc2_grad = reduce_weight(send2, keep2, "g2")
    fc1_grad = reduce_weight(send1, keep1, "g1")
    half = (rows, tokens.shape[1])
    out_own, out_other = call(restore_kernel, "k_restore", (out_rows, order), [(half, bf16)] * 2)
    out = give_back(out_own, out_other, bf16, "out")

    blockp = ((2, *proj_weight.shape), bf16)
    dh1, do, sendp, keepp, sums_two = call(
        mid_kernel,
        "k_mid",
        (da2, h1, dz, o, *wproj, col_vectors),
        [(wide, f32), (wide, bf16), blockp, blockp, ((4, width), f32)],
        scratch=[(wide, bf16)],
    )
    proj_grad = reduce_weight(sendp, keepp, "gp")
    with jax.named_scope("k_back"):
        dq, dk, dv, ds = attend_back(q, k, v, probs, do)
    blockq = ((2, qkv_weight.shape[0], 3 * qkv_weight.shape[2]), bf16)
    sendq, keepq, sums_qkv = call(
        qkv_grad_kernel,
        "k_qkvgrad",
        (a1, dq, dk, dv),
        [blockq, blockq, ((2, width), f32)],
    )
    qkv_grad = reduce_weight(sendq, keepq, "gq").reshape(qkv_weight.shape)
    g_own, g_other, sums_one = call(
        leave_kernel,
        "k_leave",
        (dq, dk, dv, dh1, x, *wqkv, col_vectors, order),
        [(half, bf16), (half, bf16), ((2, width), f32)],
        scratch=[(wide, bf16)],
    )
    grad_input = give_back(g_own, g_other, f32, "gx")

    ds_sum = ds[:, :CELLS, :CELLS] + ds[:, CELLS : 2 * CELLS, CELLS : 2 * CELLS]
    table_part = lax.dot_general(
        lookup, ds_sum.reshape(heads, -1), (((0,), (1,)), ((), ())), precision=highest
    )

    row_parts = [sums_qkv, table_part, df_sum]
    col_parts = jnp.concatenate([sums_one, sums_two], axis=0)
    row_halves = [jnp.split(p, 2, axis=1) for p in row_parts]
    col_halves = jnp.split(col_parts, 2, axis=1)
    keep_r = jnp.concatenate([h[0].reshape(-1) for h in row_halves])
    send_r = jnp.concatenate([h[1].reshape(-1) for h in row_halves])
    both_c = jnp.concatenate([h.reshape(-1) for h in col_halves])
    n_r, n_c = keep_r.shape[0], both_c.shape[0] // 2
    got = swap_row(jnp.concatenate([send_r, both_c]))
    keep_r = keep_r + got[:n_r]
    both_c = both_c + got[n_r:]
    got = swap_col(jnp.concatenate([keep_r, both_c[n_c:]]))
    small = jnp.concatenate([keep_r, both_c[:n_c]]) + got
    size = lax.axis_size("dp")
    for bit in range(size.bit_length() - 1):
        small = small + swap(small, "dp", bit)
    r_shapes = [h[0].shape for h in row_halves]
    pieces, at = [], 0
    for shape in r_shapes:
        count = shape[0] * shape[1]
        pieces.append(small[at : at + count].reshape(shape))
        at += count
    qkv_bias_grad, table_grad, fc1_bias_grad = pieces
    cols = small[n_r:].reshape(col_halves[0].shape)
    return (
        out,
        grad_input,
        qkv_grad,
        qkv_bias_grad,
        table_grad,
        proj_grad,
        cols[4],
        jnp.stack([cols[0], cols[2]]),
        jnp.stack([cols[1], cols[3]]),
        fc1_grad,
        fc1_bias_grad[0],
        fc2_grad,
        cols[5],
    )


def solution(mesh):
    return jax.shard_map(
        shards,
        mesh=mesh,
        in_specs=(
            P(("dp", "row"), "col"),
            P("col", None, "row"),
            P(None, "row"),
            P(None, "row"),
            P(),
            P(),
            P(),
            P("row", "col"),
            P("col"),
            P(None, "col"),
            P(None, "col"),
            P("col", "row"),
            P("row"),
            P("row", "col"),
            P("col"),
            P(("dp", "row"), "col"),
        ),
        out_specs=(
            P(("dp", "row"), "col"),
            P(("dp", "row"), "col"),
            P("col", None, "row"),
            P(None, "row"),
            P(None, "row"),
            P("row", "col"),
            P("col"),
            P(None, "col"),
            P(None, "col"),
            P("col", "row"),
            P("row"),
            P("row", "col"),
            P("col"),
        ),
        check_vma=False,
    )
```

```python
import functools

import jax
import jax.numpy as jnp
from jax import lax
from jax.experimental import pallas as pl
from jax.experimental.pallas import tpu as pltpu
from jax.sharding import PartitionSpec as P


HEAD_DIM = 32
WIN = 7
SIDE = 14
CELLS = WIN * WIN
IMAGE = SIDE * SIDE
PAIR = 112
GROUP = 128 // HEAD_DIM

highest = lax.Precision.HIGHEST
epsilon = 1e-05
masked_value = -1000000000.0
score_scale = HEAD_DIM ** (-0.5)
f32 = jnp.float32
bf16 = jnp.bfloat16


def swap(values, axis, bit=0):
    size = lax.axis_size(axis)
    return lax.ppermute(values, axis, [(i, i ^ (1 << bit)) for i in range(size)])


def swap_row(values):
    return swap(values, "row")


def swap_col(values):
    return swap(values, "col")


def dot(a, b):
    return jnp.dot(a, b, preferred_element_type=f32)


def dot_nt(a, b):
    return lax.dot_general(a, b, (((1,), (1,)), ((), ())), preferred_element_type=f32)


def dot_tn(a, b):
    return lax.dot_general(a, b, (((0,), (0,)), ((), ())), preferred_element_type=f32)


def lane_group():
    return lax.broadcasted_iota(jnp.int32, (PAIR, 128), 1) // HEAD_DIM


def fill_lanes(rows):
    return jnp.concatenate([rows, jnp.zeros((128 - PAIR, 128), rows.dtype)], axis=0)


def stack_heads(rows, lanes):
    zero = jnp.zeros_like(rows)
    return jnp.concatenate([jnp.where(lanes == j, rows, zero) for j in range(GROUP)], axis=0)


def pick_heads(parts, lanes):
    total = parts[0]
    for j in range(1, GROUP):
        total = jnp.where(lanes == j, parts[j], total)
    return total


def attend_kernel(q_ref, k_ref, v_ref, bias_ref, p_ref, o_ref):
    lanes = lane_group()

    @pl.loop(0, q_ref.shape[0] // PAIR)
    def _(i):
        rows = pl.ds(pl.multiple_of(i * PAIR, PAIR), PAIR)
        for g in range(bias_ref.shape[1] // GROUP):
            cols = slice(g * 128, (g + 1) * 128)
            heads = slice(g * GROUP, (g + 1) * GROUP)
            v = v_ref[rows, cols]
            s = dot_nt(stack_heads(k_ref[rows, cols], lanes), fill_lanes(q_ref[rows, cols]))
            s = s.reshape(GROUP, PAIR, 128) * score_scale + bias_ref[lax.rem(i, 2), heads]
            e = jnp.exp(s - jnp.max(s, axis=1, keepdims=True))
            p = (e * (1.0 / jnp.sum(e, axis=1, keepdims=True))).astype(bf16)
            p_ref[i, heads] = p
            o_ref[rows, cols] = pick_heads(
                [dot_tn(p[j], v)[:PAIR] for j in range(GROUP)], lanes
            ).astype(bf16)


def attend_back_kernel(q_ref, k_ref, v_ref, p_ref, do_ref, dq_ref, dk_ref, dv_ref, ds_ref):
    lanes = lane_group()
    ds_ref[...] = jnp.zeros_like(ds_ref)

    @pl.loop(0, q_ref.shape[0] // PAIR)
    def _(i):
        rows = pl.ds(pl.multiple_of(i * PAIR, PAIR), PAIR)
        for g in range(p_ref.shape[1] // GROUP):
            cols = slice(g * 128, (g + 1) * 128)
            heads = slice(g * GROUP, (g + 1) * GROUP)
            k = k_ref[rows, cols]
            q = fill_lanes(q_ref[rows, cols])
            do = fill_lanes(do_ref[rows, cols])
            p = p_ref[i, heads]
            pf = p.astype(f32)
            dp = dot_nt(stack_heads(v_ref[rows, cols], lanes), do).reshape(GROUP, PAIR, 128)
            ds = (pf * (dp - jnp.sum(pf * dp, axis=1, keepdims=True))).astype(bf16)
            ds_ref[heads] += ds.astype(f32)
            dk = dot(ds.reshape(GROUP * PAIR, 128), q).reshape(GROUP, PAIR, 128)
            dv = dot(p.reshape(GROUP * PAIR, 128), do).reshape(GROUP, PAIR, 128)
            dq = [dot_tn(ds[j], k)[:PAIR] for j in range(GROUP)]
            dq_ref[rows, cols] = (pick_heads(dq, lanes) * score_scale).astype(bf16)
            dk_ref[rows, cols] = (pick_heads(dk, lanes) * score_scale).astype(bf16)
            dv_ref[rows, cols] = pick_heads(dv, lanes).astype(bf16)


def table_kernel(ds_ref, index_ref, out_ref):
    entries = lax.broadcasted_iota(jnp.int32, (HALF, 128), 0)
    heads = ds_ref.shape[0]
    out_ref[...] = jnp.zeros_like(out_ref)

    @pl.loop(0, CELLS // WIN)
    def _(step):
        base = step * 2 * WIN
        total = jnp.zeros((2 * heads, HALF), f32)
        for pair in range(WIN):
            parts, hits = [], []
            for one in range(2):
                at = pl.ds(base + 2 * pair + one, 1)
                ds = ds_ref[:, at, :].reshape(heads, 128)
                high = ds.astype(bf16)
                low = (ds - high.astype(f32)).astype(bf16)
                parts.append(jnp.concatenate([high, low], axis=0))
                hits.append((entries == index_ref[at, :]).astype(f32).astype(bf16))
            total = total + dot_nt(jnp.concatenate(parts, axis=1), jnp.concatenate(hits, axis=1))
        out_ref[...] += total[:heads] + total[heads:]


def chunked(rows, body):
    @pl.loop(0, rows // PAIR)
    def _(i):
        body(pl.ds(pl.multiple_of(i * PAIR, PAIR), PAIR))


def standardize(values):
    center = jnp.mean(values, axis=1, keepdims=True)
    centered = values - center
    scaling = lax.rsqrt(jnp.mean(centered * centered, axis=1, keepdims=True) + epsilon)
    return centered * scaling, scaling


def standardize_back(grad, hat, scaling, gain):
    scaled = grad * gain
    first = jnp.mean(scaled, axis=1, keepdims=True)
    second = jnp.mean(scaled * hat, axis=1, keepdims=True)
    return scaling * (scaled - first - hat * second)


def add_sum(ref, row, values):
    ref[row : row + 1, :] += jnp.sum(values, axis=0, keepdims=True)


GAIN1, GAIN2, SHIFT1, SHIFT2, BIAS_PROJ, BIAS_FC2 = range(6)
HALF = 256


def enter_kernel(side_in, own_ref, other_ref, order_ref, vec_ref, x_ref, a_ref, side_ref):
    for bit in range(side_in.shape[0]):
        side_ref[bit] = side_in[bit]
    images = own_ref.shape[0] // IMAGE
    for n in range(images):
        rows = slice(n * IMAGE, (n + 1) * IMAGE)
        tok = jnp.concatenate([own_ref[rows], other_ref[rows]], axis=1)
        x = dot(order_ref[...], tok)
        hat, _ = standardize(x)
        a = hat * vec_ref[GAIN1 : GAIN1 + 1] + vec_ref[SHIFT1 : SHIFT1 + 1]
        out = slice(n * 2 * PAIR, (n + 1) * 2 * PAIR)
        x_ref[out] = x.astype(bf16)
        a_ref[out] = a.astype(bf16)


def qkv_kernel(a_ref, w0, w1, w2, w3, bias_ref, q_ref, k_ref, v_ref):
    for side, (top, low) in enumerate(((w0, w2), (w1, w3))):
        cols = slice(side * HALF, (side + 1) * HALF)
        for j, ref in enumerate((q_ref, k_ref, v_ref)):
            y = dot(a_ref[:, :HALF], top[j]) + dot(a_ref[:, HALF:], low[j])
            if j != 1:
                y = y + bias_ref[j // 2 : j // 2 + 1, cols]
            ref[:, cols] = y.astype(bf16)


def proj_kernel(x_ref, o_ref, w0, w1, w2, w3, vec_ref, h_ref, a_ref):
    def body(rows):
        o0, o1 = o_ref[rows, :HALF], o_ref[rows, HALF:]
        y = jnp.concatenate(
            [dot(o0, w0[...]) + dot(o1, w1[...]), dot(o0, w2[...]) + dot(o1, w3[...])], axis=1
        )
        h = x_ref[rows].astype(f32) + y + vec_ref[BIAS_PROJ : BIAS_PROJ + 1]
        hat, _ = standardize(h)
        h_ref[rows] = h
        a_ref[rows] = (
            hat * vec_ref[GAIN2 : GAIN2 + 1] + vec_ref[SHIFT2 : SHIFT2 + 1]
        ).astype(bf16)

    chunked(x_ref.shape[0], body)


def mlp_kernel(*refs):
    side_ref, a_ref, dz_ref, h_ref, bias_ref, vec_ref = refs[:6]
    u, w = refs[6:12], refs[12:18]
    out_ref, da_ref, send2_ref, keep2_ref, send1_ref, keep1_ref, bsum_ref = refs[18:25]
    acc_ref, at_ref = refs[25:]
    hidden = u[0].shape[1]
    near = hidden // HALF // 2
    at_ref[...] = a_ref[...].T
    acc_ref[...] = h_ref[...] + vec_ref[BIAS_FC2 : BIAS_FC2 + 1]
    da_ref[...] = jnp.zeros_like(da_ref)
    z0, z1 = dz_ref[:, :HALF], dz_ref[:, HALF:]

    for side, grad2, grad1 in ((1, send2_ref, send1_ref), (0, keep2_ref, keep1_ref)):
        for half in range(2):
            up, down = u[2 + 2 * side + half], w[2 + 2 * side + half]
            first = (side_ref[0] if half == 0 else 1 - side_ref[0]) * near

            @pl.loop(0, near)
            def _(t, side=side, grad2=grad2, grad1=grad1, up=up, down=down, first=first):
                here = pl.ds(pl.multiple_of(t * HALF, HALF), HALF)
                tile = pl.ds(pl.multiple_of((first + t) * HALF, HALF), HALF)
                where = pl.ds(pl.multiple_of(side * hidden + (first + t) * HALF, HALF), HALF)
                p0, p1 = u[side][:, tile], up[:, here]
                d0, d1 = w[side][tile], down[here]
                f = dot(a_ref[:, :HALF], p0) + dot(a_ref[:, HALF:], p1) + bias_ref[:, where]
                dm = dot_nt(z0, d0) + dot_nt(z1, d1)
                cdf = 0.5 * (1.0 + lax.erf(f * (0.5**0.5)))
                m = (f * cdf).astype(bf16)
                slope = cdf + f * (jnp.exp(-0.5 * f * f) * 0.3989422804014327)
                df = (dm * slope).astype(bf16)
                bsum_ref[:, where] = jnp.sum(df.astype(f32), axis=0, keepdims=True)
                acc_ref[:, :HALF] += dot(m, d0)
                acc_ref[:, HALF:] += dot(m, d1)
                da_ref[:, :HALF] += dot_nt(df, p0)
                da_ref[:, HALF:] += dot_nt(df, p1)
                mt = m.T
                grad2[0, tile] = dot(mt, z0).astype(bf16)
                grad2[1, tile] = dot(mt, z1).astype(bf16)
                grad1[0, tile] = dot(at_ref[:HALF], df).astype(bf16)
                grad1[1, tile] = dot(at_ref[HALF:], df).astype(bf16)

    out_ref[...] = acc_ref[...].astype(bf16)


def mid_kernel(
    da_ref, h_ref, dz_ref, o_ref, w0, w1, w2, w3, vec_ref, dh_ref, do_ref, send_ref, keep_ref, sum_ref, dy_ref
):
    sum_ref[...] = jnp.zeros_like(sum_ref)

    def body(rows):
        hat, scaling = standardize(h_ref[rows])
        da = da_ref[rows]
        dz = dz_ref[rows].astype(f32)
        du = standardize_back(da, hat, scaling, vec_ref[GAIN2 : GAIN2 + 1])
        dh = dz + du
        dh_ref[rows] = dh
        dy = dh.astype(bf16)
        dy_ref[rows] = dy
        y0, y1 = dy[:, :HALF], dy[:, HALF:]
        do_ref[rows] = jnp.concatenate(
            [dot_nt(y0, w0[...]) + dot_nt(y1, w2[...]), dot_nt(y0, w1[...]) + dot_nt(y1, w3[...])],
            axis=1,
        ).astype(bf16)
        add_sum(sum_ref, 0, da * hat)
        add_sum(sum_ref, 1, da)
        add_sum(sum_ref, 2, dy.astype(f32))
        add_sum(sum_ref, 3, dz)

    chunked(h_ref.shape[0], body)
    ot = o_ref[...].T
    for side, ref in enumerate((keep_ref, send_ref)):
        for c in range(2):
            ref[c] = dot(
                ot[side * HALF : (side + 1) * HALF], dy_ref[:, c * HALF : (c + 1) * HALF]
            ).astype(bf16)


def qkv_grad_kernel(a_ref, dq_ref, dk_ref, dv_ref, sendp_ref, keepp_ref, send_ref, keep_ref, sum_ref):
    at = a_ref[...].T
    for side, (ref, proj_ref) in enumerate(((keep_ref, keepp_ref), (send_ref, sendp_ref))):
        cols = slice(side * HALF, (side + 1) * HALF)
        ref[:, 3 * HALF :] = proj_ref[...]
        for j, d_ref in enumerate((dq_ref, dk_ref, dv_ref)):
            d = d_ref[:, cols]
            for c in range(2):
                ref[c, j * HALF : (j + 1) * HALF] = dot(at[c * HALF : (c + 1) * HALF], d).astype(bf16)
            if j != 1:
                sum_ref[j // 2 : j // 2 + 1, cols] = jnp.sum(d.astype(f32), axis=0, keepdims=True)


def leave_kernel(
    dq_ref, dk_ref, dv_ref, dh_ref, x_ref, w0, w1, w2, w3, vec_ref, order_ref, own_ref, other_ref, sum_ref, g_ref
):
    sum_ref[...] = jnp.zeros_like(sum_ref)

    def body(rows):
        da = []
        for top, low in ((w0, w1), (w2, w3)):
            part = None
            for j, ref in enumerate((dq_ref, dk_ref, dv_ref)):
                y = dot_nt(ref[rows, :HALF], top[j]) + dot_nt(ref[rows, HALF:], low[j])
                part = y if part is None else part + y
            da.append(part)
        da = jnp.concatenate(da, axis=1)
        hat, scaling = standardize(x_ref[rows].astype(f32))
        du = standardize_back(da, hat, scaling, vec_ref[GAIN1 : GAIN1 + 1])
        g_ref[rows] = (dh_ref[rows] + du).astype(bf16)
        add_sum(sum_ref, 0, da * hat)
        add_sum(sum_ref, 1, da)

    chunked(x_ref.shape[0], body)
    restore(g_ref, order_ref, own_ref, other_ref)


def restore(rows_ref, order_ref, own_ref, other_ref):
    images = own_ref.shape[0] // IMAGE
    for n in range(images):
        g = dot_tn(order_ref[...], rows_ref[n * 2 * PAIR : (n + 1) * 2 * PAIR])
        out = slice(n * IMAGE, (n + 1) * IMAGE)
        own_ref[out] = g[:, :HALF].astype(bf16)
        other_ref[out] = g[:, HALF:].astype(bf16)


def restore_kernel(rows_ref, order_ref, own_ref, other_ref):
    restore(rows_ref, order_ref, own_ref, other_ref)


def arrange_kernel(own_ref, other_ref, order_ref, out_ref):
    images = own_ref.shape[0] // IMAGE
    for n in range(images):
        rows = slice(n * IMAGE, (n + 1) * IMAGE)
        tok = jnp.concatenate([own_ref[rows], other_ref[rows]], axis=1)
        out_ref[n * 2 * PAIR : (n + 1) * 2 * PAIR] = dot(order_ref[...], tok).astype(bf16)


def row_add_kernel(keep_ref, got_ref, own_ref, away_ref):
    own_ref[...] = keep_ref[0] + got_ref[0]
    away_ref[...] = keep_ref[1] + got_ref[1]


def halve_kernel(bit, side_ref, own_ref, got_ref, mine_ref, away_ref):
    half = mine_ref.shape[-2]
    lead = (slice(None),) * (len(mine_ref.shape) - 2)
    for out_ref, at in ((mine_ref, side_ref[bit]), (away_ref, 1 - side_ref[bit])):
        rows = (*lead, pl.ds(pl.multiple_of(at * half, half), half))
        out_ref[...] = own_ref[rows] + got_ref[rows]


def add_kernel(own_ref, got_ref, out_ref):
    out_ref[...] = own_ref[...] + got_ref[...]


def double_kernel(bit, side_ref, own_ref, got_ref, out_ref):
    half = own_ref.shape[0]
    for ref, at in ((own_ref, side_ref[bit]), (got_ref, 1 - side_ref[bit])):
        out_ref[pl.ds(pl.multiple_of(at * half, half), half)] = ref[...]


def last_fc2_kernel(side_ref, own_ref, got_ref, out_ref):
    half = own_ref.shape[0]
    for ref, at in ((own_ref, side_ref[0]), (got_ref, 1 - side_ref[0])):
        out_ref[pl.ds(pl.multiple_of(at * half, half), half)] = ref[...].astype(f32)


def last_fc1_kernel(side_ref, own_ref, got_ref, out_ref):
    tiles = own_ref.shape[0] // HALF
    for ref, at in ((own_ref, side_ref[0]), (got_ref, 1 - side_ref[0])):
        for t in range(tiles):
            lanes = pl.ds(pl.multiple_of((at * tiles + t) * HALF, HALF), HALF)
            out_ref[:, lanes] = ref[t * HALF : (t + 1) * HALF].astype(f32)


def last_qkv_kernel(side_ref, own_ref, got_ref, qkv_ref, proj_ref):
    def place(low, high):
        qkv_ref[0] = low[:HALF].astype(f32)
        qkv_ref[1] = low[HALF:].astype(f32)
        qkv_ref[2] = high[:HALF].astype(f32)
        proj_ref[...] = high[HALF:].astype(f32)

    @pl.when(side_ref[0] == 0)
    def _():
        place(own_ref, got_ref)

    @pl.when(side_ref[0] != 0)
    def _():
        place(got_ref, own_ref)


SPLIT, FEATURES = 14, 6


def pack_kernel(qkv_ref, fc1_ref, table_ref, one_ref, two_ref, send_ref, keep_ref):
    for side, ref in enumerate((keep_ref, send_ref)):
        cols = slice(side * HALF, (side + 1) * HALF)
        ref[...] = jnp.zeros_like(ref)
        ref[0:2] = qkv_ref[:, cols]
        for t in range(4):
            at = (side * 4 + t) * HALF
            ref[2 + t : 3 + t] = fc1_ref[:, at : at + HALF]
        ref[6:SPLIT] = table_ref[side * 8 : side * 8 + 8]
        for c in range(2):
            at, half = SPLIT + c * FEATURES, slice(c * HALF, (c + 1) * HALF)
            ref[at : at + 2] = one_ref[:, half]
            ref[at + 2 : at + 6] = two_ref[:, half]


def small_row_kernel(keep_ref, got_ref, own_ref, away_ref):
    total = keep_ref[...] + got_ref[...]
    end = SPLIT + FEATURES
    for ref, at in ((own_ref, SPLIT), (away_ref, end)):
        ref[...] = jnp.zeros_like(ref)
        ref[:SPLIT] = total[:SPLIT]
        ref[SPLIT:end] = total[at : at + FEATURES]


def unpack_kernel(own_ref, got_ref, qkv_ref, fc1_ref, table_ref, gain_ref, shift_ref, proj_ref, fc2_ref):
    total = own_ref[...] + got_ref[...]
    qkv_ref[...] = total[0:2]
    for t in range(4):
        fc1_ref[:, t * HALF : (t + 1) * HALF] = total[2 + t : 3 + t]
    table_ref[...] = total[6:SPLIT].T[: table_ref.shape[0]]
    for j in range(2):
        gain_ref[j : j + 1] = total[SPLIT + 2 * j : SPLIT + 2 * j + 1]
        shift_ref[j : j + 1] = total[SPLIT + 2 * j + 1 : SPLIT + 2 * j + 2]
    proj_ref[...] = total[SPLIT + 4 : SPLIT + 5]
    fc2_ref[...] = total[SPLIT + 5 : SPLIT + 6]


def call(kernel, args, outs, scratch=(), flops=10**9, vmem=4):
    def space(dtype):
        whole_numbers = dtype == jnp.int32
        return pl.BlockSpec(memory_space=pltpu.SMEM if whole_numbers else pltpu.VMEM)

    return pl.pallas_call(
        kernel,
        in_specs=[
            pl.BlockSpec(memory_space=pltpu.SMEM if a.dtype == jnp.int32 and a.ndim == 1 else pltpu.VMEM)
            for a in args
        ],
        out_specs=[space(dtype) for _, dtype in outs],
        out_shape=[jax.ShapeDtypeStruct(shape, dtype) for shape, dtype in outs],
        scratch_shapes=[pltpu.VMEM(shape, dtype) for shape, dtype in scratch],
        cost_estimate=pl.CostEstimate(flops=flops, bytes_accessed=4 * 10**6, transcendentals=0),
        compiler_params=pltpu.CompilerParams(vmem_limit_bytes=vmem << 20),
    )(*args)


def both_cols(vector):
    return jnp.concatenate([vector, swap_col(vector)], axis=-1)


def both_rows(vector):
    return jnp.concatenate([vector, swap_row(vector)], axis=-1)


def gather_weight(weight):
    mine = swap_row(weight)
    other = swap_col(weight)
    return weight, mine, other, swap_row(other)


def relay_weight(half):
    near = swap_col(half)
    far = swap(near, "dp") if lax.axis_size("dp") > 1 else near
    near_row = swap_row(near)
    far_row = swap_row(far)
    return near, far, near_row, far_row


def reduce_weight(send, keep, sides, first_bit, last, outs):
    bits = lax.axis_size("dp").bit_length() - 1
    halved = bits - 1
    small = 10**8

    def halve(own, got, bit):
        shape = own.shape[:-2] + (own.shape[-2] // 2, own.shape[-1])
        own, away = call(
            functools.partial(halve_kernel, bit),
            (sides, own, got),
            [(shape, bf16)] * 2,
            flops=small,
        )
        return own, swap(away, "dp", bit)

    got = swap_row(send)
    own, start = keep, 0
    if first_bit:
        own, got = halve(own, got, 0)
        start = 1
    own, away = call(row_add_kernel, (own, got), [(own.shape[1:], bf16)] * 2, flops=small)
    got = swap_col(away)
    for bit in range(start, halved):
        own, got = halve(own, got, bit)
    for bit in (bits - 1,):
        (own,) = call(add_kernel, (own, got), [(own.shape, bf16)], flops=small)
        got = swap(own, "dp", bit)
    (own,) = call(add_kernel, (own, got), [(own.shape, bf16)], flops=small)
    for bit in reversed(range(halved)):
        got = swap(own, "dp", bit)
        if bit:
            (own,) = call(
                functools.partial(double_kernel, bit),
                (sides, own, got),
                [((2 * own.shape[0], own.shape[1]), bf16)],
                flops=small,
            )
    return call(last, (sides, own, got), outs, flops=small)


def shards(
    tokens,
    qkv_weight,
    qkv_bias,
    pos_table,
    rel_index,
    region_ids,
    shifts,
    proj_weight,
    proj_bias,
    layer_norm_scales,
    layer_norm_biases,
    fc1_weight,
    fc1_bias,
    fc2_weight,
    fc2_bias,
    cotangent,
):
    col = lax.axis_index("col")
    me = lax.axis_index("dp")
    bits = lax.axis_size("dp").bit_length() - 1
    rows = tokens.shape[0] // 2
    side = (me & 1) if bits else 0

    def exchange(values):
        keep = lax.dynamic_slice_in_dim(values, col * rows, rows, 0)
        send = lax.dynamic_slice_in_dim(values, (1 - col) * rows, rows, 0)
        return keep, swap_col(send)

    def give_back(keep, send, dtype):
        other = swap_col(send)
        keep, other = keep.astype(dtype), other.astype(dtype)
        return jnp.where(
            col == 0,
            jnp.concatenate([keep, other], axis=0),
            jnp.concatenate([other, keep], axis=0),
        )

    def halved(weight, dim):
        size = weight.shape[dim] // 2
        return lax.dynamic_slice_in_dim(weight, side * size, size, dim)

    def with_row(weight):
        return weight, swap_row(weight)

    x_own, x_other = exchange(tokens)
    wqkv = gather_weight(qkv_weight.transpose(1, 0, 2))
    wproj = gather_weight(proj_weight)
    wfc1 = (*with_row(fc1_weight), *relay_weight(halved(fc1_weight, 1)))
    wfc2 = (*with_row(fc2_weight), *relay_weight(halved(fc2_weight, 0)))
    z_own, z_other = exchange(cotangent)
    vectors = both_cols(
        jnp.stack(
            [
                layer_norm_scales[0],
                layer_norm_scales[1],
                layer_norm_biases[0],
                layer_norm_biases[1],
                proj_bias,
                fc2_bias,
            ]
        ),
    )
    bias_fc1 = both_rows(fc1_bias)
    bias_qkv = both_rows(qkv_bias)
    table = both_rows(pos_table)
    entries, heads = table.shape
    sides_in = jnp.stack([(me >> bit) & 1 for bit in range(max(bits, 1))]).astype(jnp.int32)

    place = jnp.arange(2 * PAIR, dtype=jnp.int32)
    pair, inside = place // PAIR, place % PAIR
    window = 2 * pair + inside // CELLS
    spot = inside % CELLS
    cell_i = (window // 2) * WIN + spot // WIN
    cell_j = (window % 2) * WIN + spot % WIN
    token = ((cell_i + shifts[0]) % SIDE) * SIDE + (cell_j + shifts[1]) % SIDE
    token = jnp.where(inside < 2 * CELLS, token, -1)
    order = (token[:, None] == jnp.arange(IMAGE, dtype=jnp.int32)[None, :]).astype(bf16)

    index_t = rel_index.T
    lookup = (index_t.reshape(-1)[:, None] == jnp.arange(entries)[None, :]).astype(f32)
    pos = jnp.dot(lookup, table, precision=highest).T.reshape(heads, CELLS, CELLS)
    per_side = SIDE // WIN
    zones = region_ids.reshape(per_side, WIN, per_side, WIN).transpose(0, 2, 1, 3)
    zones = zones.reshape(per_side * per_side, CELLS)
    allowed = zones[:, :, None] == zones[:, None, :]
    biased = jnp.where(allowed[:, None], pos[None], masked_value)

    def corner(values, low, fill):
        high = PAIR - low - CELLS
        pad = [(0, 0)] * (values.ndim - 2) + [(low, high), (low, high + 128 - PAIR)]
        return jnp.pad(values, pad, constant_values=fill)

    bias = jnp.maximum(
        corner(biased[0::2], 0, masked_value), corner(biased[1::2], CELLS, masked_value)
    )
    pair_index = jnp.maximum(corner(index_t, 0, -1), corner(index_t, CELLS, -1))

    count = rows // IMAGE * 2 * PAIR
    width = 2 * tokens.shape[1]
    wide = (count, width)
    x, a1, sides = call(
        enter_kernel,
        (sides_in, x_own, x_other, order, vectors),
        [(wide, bf16), (wide, bf16), (sides_in.shape, jnp.int32)],
    )
    q, k, v = call(qkv_kernel, (a1, *wqkv, bias_qkv), [(wide, bf16)] * 3)
    probs, o = call(
        attend_kernel,
        (q, k, v, bias),
        [((count // PAIR, heads, PAIR, 128), bf16), (wide, bf16)],
        vmem=8,
    )
    h1, a2 = call(proj_kernel, (x, o, *wproj, vectors), [(wide, f32), (wide, bf16)])
    (dz,) = call(arrange_kernel, (z_own, z_other, order), [(wide, bf16)])
    block = ((2, 4 * HALF, HALF), bf16)
    out_rows, da2, send2, keep2, send1, keep1, df_sum = call(
        mlp_kernel,
        (sides, a2, dz, h1, bias_fc1[None], vectors, *wfc1, *wfc2),
        [
            (wide, bf16),
            (wide, f32),
            block,
            block,
            block,
            block,
            ((1, bias_fc1.shape[0]), f32),
        ],
        scratch=[(wide, f32), (wide[::-1], bf16)],
        flops=3 * 10**9,
        vmem=8,
    )
    (fc2_grad,) = reduce_weight(
        send2, keep2, sides, False, last_fc2_kernel, [(fc2_weight.shape, f32)]
    )
    (fc1_grad,) = reduce_weight(
        send1, keep1, sides, True, last_fc1_kernel, [(fc1_weight.shape, f32)]
    )
    half = (rows, tokens.shape[1])
    out_own, out_other = call(restore_kernel, (out_rows, order), [(half, bf16)] * 2)
    out = give_back(out_own, out_other, bf16)

    blockp = ((2, *proj_weight.shape), bf16)
    dh1, do, sendp, keepp, sums_two = call(
        mid_kernel,
        (da2, h1, dz, o, *wproj, vectors),
        [(wide, f32), (wide, bf16), blockp, blockp, ((4, width), f32)],
        scratch=[(wide, bf16)],
    )
    dq, dk, dv, ds = call(
        attend_back_kernel,
        (q, k, v, probs, do),
        [(wide, bf16)] * 3 + [((heads, PAIR, 128), f32)],
        vmem=8,
    )
    sendq, keepq, sums_qkv = call(
        qkv_grad_kernel, (a1, dq, dk, dv, sendp, keepp), [block, block, ((2, width), f32)]
    )
    qkv_grad, proj_grad = reduce_weight(
        sendq,
        keepq,
        sides,
        False,
        last_qkv_kernel,
        [((3, HALF, HALF), f32), (proj_weight.shape, f32)],
    )
    g_own, g_other, sums_one = call(
        leave_kernel,
        (dq, dk, dv, dh1, x, *wqkv, vectors, order),
        [(half, bf16), (half, bf16), ((2, width), f32)],
        scratch=[(wide, bf16)],
    )
    grad_input = give_back(g_own, g_other, f32)

    (table_sums,) = call(table_kernel, (ds, pair_index), [((heads, HALF), f32)])
    small = ((32, HALF), f32)
    sent, own = call(pack_kernel, (sums_qkv, df_sum, table_sums, sums_one, sums_two), [small] * 2)
    got = swap_row(sent)
    small = ((24, HALF), f32)
    own, away = call(small_row_kernel, (own, got), [small] * 2)
    got = swap_col(away)
    for bit in range(bits):
        (own,) = call(add_kernel, (own, got), [small])
        got = swap(own, "dp", bit)
    qkv_bias_grad, fc1_bias_grad, table_grad, gains, shifted, proj_bias_grad, fc2_bias_grad = call(
        unpack_kernel,
        (own, got),
        [
            ((2, HALF), f32),
            ((1, fc1_bias.shape[0]), f32),
            (pos_table.shape, f32),
            ((2, HALF), f32),
            ((2, HALF), f32),
            ((1, HALF), f32),
            ((1, HALF), f32),
        ],
    )
    return (
        out,
        grad_input,
        qkv_grad.transpose(1, 0, 2),
        qkv_bias_grad,
        table_grad,
        proj_grad,
        proj_bias_grad[0],
        gains,
        shifted,
        fc1_grad,
        fc1_bias_grad[0],
        fc2_grad,
        fc2_bias_grad[0],
    )


def solution(mesh):
    return jax.shard_map(
        shards,
        mesh=mesh,
        in_specs=(
            P(("dp", "row"), "col"),
            P("col", None, "row"),
            P(None, "row"),
            P(None, "row"),
            P(),
            P(),
            P(),
            P("row", "col"),
            P("col"),
            P(None, "col"),
            P(None, "col"),
            P("col", "row"),
            P("row"),
            P("row", "col"),
            P("col"),
            P(("dp", "row"), "col"),
        ),
        out_specs=(
            P(("dp", "row"), "col"),
            P(("dp", "row"), "col"),
            P("col", None, "row"),
            P(None, "row"),
            P(None, "row"),
            P("row", "col"),
            P("col"),
            P(None, "col"),
            P(None, "col"),
            P("col", "row"),
            P("row"),
            P("row", "col"),
            P("col"),
        ),
        check_vma=False,
    )
```

```python
import functools

import jax
import jax.numpy as jnp
from jax import lax
from jax.experimental import pallas as pl
from jax.experimental.pallas import tpu as pltpu
from jax.sharding import PartitionSpec as P


HEAD_DIM = 32
WIN = 7
SIDE = 14
CELLS = WIN * WIN
IMAGE = SIDE * SIDE
PAIR = 112
GROUP = 128 // HEAD_DIM

highest = lax.Precision.HIGHEST
epsilon = 1e-05
masked_value = -1000000000.0
score_scale = HEAD_DIM ** (-0.5)
f32 = jnp.float32
bf16 = jnp.bfloat16


def swap(values, axis, bit=0):
    size = lax.axis_size(axis)
    return lax.ppermute(values, axis, [(i, i ^ (1 << bit)) for i in range(size)])


def swap_row(values):
    return swap(values, "row")


def swap_col(values):
    return swap(values, "col")


def dot(a, b):
    return jnp.dot(a, b, preferred_element_type=f32)


def dot_nt(a, b):
    return lax.dot_general(a, b, (((1,), (1,)), ((), ())), preferred_element_type=f32)


def dot_tn(a, b):
    return lax.dot_general(a, b, (((0,), (0,)), ((), ())), preferred_element_type=f32)


def lane_group():
    return lax.broadcasted_iota(jnp.int32, (PAIR, 128), 1) // HEAD_DIM


def fill_lanes(rows):
    return jnp.concatenate([rows, jnp.zeros((128 - PAIR, 128), rows.dtype)], axis=0)


def stack_heads(rows, lanes):
    zero = jnp.zeros_like(rows)
    return jnp.concatenate([jnp.where(lanes == j, rows, zero) for j in range(GROUP)], axis=0)


def pick_heads(parts, lanes):
    total = parts[0]
    for j in range(1, GROUP):
        total = jnp.where(lanes == j, parts[j], total)
    return total


def attend_kernel(q_ref, k_ref, v_ref, bias_ref, p_ref, o_ref):
    lanes = lane_group()

    @pl.loop(0, q_ref.shape[0] // PAIR)
    def _(i):
        rows = pl.ds(pl.multiple_of(i * PAIR, PAIR), PAIR)
        for g in range(bias_ref.shape[1] // GROUP):
            cols = slice(g * 128, (g + 1) * 128)
            heads = slice(g * GROUP, (g + 1) * GROUP)
            v = v_ref[rows, cols]
            s = dot_nt(stack_heads(k_ref[rows, cols], lanes), fill_lanes(q_ref[rows, cols]))
            s = s.reshape(GROUP, PAIR, 128) * score_scale + bias_ref[lax.rem(i, 2), heads]
            e = jnp.exp(s - jnp.max(s, axis=1, keepdims=True))
            p = (e * (1.0 / jnp.sum(e, axis=1, keepdims=True))).astype(bf16)
            p_ref[i, heads] = p
            o_ref[rows, cols] = pick_heads(
                [dot_tn(p[j], v)[:PAIR] for j in range(GROUP)], lanes
            ).astype(bf16)


def attend_back_kernel(q_ref, k_ref, v_ref, p_ref, do_ref, dq_ref, dk_ref, dv_ref, ds_ref):
    lanes = lane_group()
    ds_ref[...] = jnp.zeros_like(ds_ref)

    @pl.loop(0, q_ref.shape[0] // PAIR)
    def _(i):
        rows = pl.ds(pl.multiple_of(i * PAIR, PAIR), PAIR)
        for g in range(p_ref.shape[1] // GROUP):
            cols = slice(g * 128, (g + 1) * 128)
            heads = slice(g * GROUP, (g + 1) * GROUP)
            k = k_ref[rows, cols]
            q = fill_lanes(q_ref[rows, cols])
            do = fill_lanes(do_ref[rows, cols])
            p = p_ref[i, heads]
            pf = p.astype(f32)
            dp = dot_nt(stack_heads(v_ref[rows, cols], lanes), do).reshape(GROUP, PAIR, 128)
            ds = (pf * (dp - jnp.sum(pf * dp, axis=1, keepdims=True))).astype(bf16)
            ds_ref[heads] += ds.astype(f32)
            dk = dot(ds.reshape(GROUP * PAIR, 128), q).reshape(GROUP, PAIR, 128)
            dv = dot(p.reshape(GROUP * PAIR, 128), do).reshape(GROUP, PAIR, 128)
            dq = [dot_tn(ds[j], k)[:PAIR] for j in range(GROUP)]
            dq_ref[rows, cols] = (pick_heads(dq, lanes) * score_scale).astype(bf16)
            dk_ref[rows, cols] = (pick_heads(dk, lanes) * score_scale).astype(bf16)
            dv_ref[rows, cols] = pick_heads(dv, lanes).astype(bf16)


def table_kernel(ds_ref, index_ref, out_ref):
    entries = lax.broadcasted_iota(jnp.int32, (HALF, 128), 0)
    heads = ds_ref.shape[0]
    out_ref[...] = jnp.zeros_like(out_ref)

    @pl.loop(0, CELLS // WIN)
    def _(step):
        base = step * 2 * WIN
        total = jnp.zeros((2 * heads, HALF), f32)
        for pair in range(WIN):
            parts, hits = [], []
            for one in range(2):
                at = pl.ds(base + 2 * pair + one, 1)
                ds = ds_ref[:, at, :].reshape(heads, 128)
                high = ds.astype(bf16)
                low = (ds - high.astype(f32)).astype(bf16)
                parts.append(jnp.concatenate([high, low], axis=0))
                hits.append((entries == index_ref[at, :]).astype(f32).astype(bf16))
            total = total + dot_nt(jnp.concatenate(parts, axis=1), jnp.concatenate(hits, axis=1))
        out_ref[...] += total[:heads] + total[heads:]


def chunked(rows, body):
    @pl.loop(0, rows // PAIR)
    def _(i):
        body(pl.ds(pl.multiple_of(i * PAIR, PAIR), PAIR))


def standardize(values):
    center = jnp.mean(values, axis=1, keepdims=True)
    centered = values - center
    scaling = lax.rsqrt(jnp.mean(centered * centered, axis=1, keepdims=True) + epsilon)
    return centered * scaling, scaling


def standardize_back(grad, hat, scaling, gain):
    scaled = grad * gain
    first = jnp.mean(scaled, axis=1, keepdims=True)
    second = jnp.mean(scaled * hat, axis=1, keepdims=True)
    return scaling * (scaled - first - hat * second)


def add_sum(ref, row, values):
    ref[row : row + 1, :] += jnp.sum(values, axis=0, keepdims=True)


ROW_FLAG = 7
GAIN1, GAIN2, SHIFT1, SHIFT2, BIAS_PROJ, BIAS_FC2 = range(6)
HALF = 256


def enter_kernel(side_in, own_ref, other_ref, order_ref, vec_ref, x_ref, a_ref, side_ref):
    side_ref[...] = side_in[...]
    images = own_ref.shape[0] // IMAGE
    for n in range(images):
        rows = slice(n * IMAGE, (n + 1) * IMAGE)
        tok = jnp.concatenate([own_ref[rows], other_ref[rows]], axis=1)
        x = dot(order_ref[...], tok)
        hat, _ = standardize(x)
        a = hat * vec_ref[GAIN1 : GAIN1 + 1] + vec_ref[SHIFT1 : SHIFT1 + 1]
        out = slice(n * 2 * PAIR, (n + 1) * 2 * PAIR)
        x_ref[out] = x.astype(bf16)
        a_ref[out] = a.astype(bf16)


def qkv_kernel(a_ref, w0, w1, w2, w3, bias_ref, q_ref, k_ref, v_ref):
    for side, (top, low) in enumerate(((w0, w2), (w1, w3))):
        cols = slice(side * HALF, (side + 1) * HALF)
        for j, ref in enumerate((q_ref, k_ref, v_ref)):
            y = dot(a_ref[:, :HALF], top[j]) + dot(a_ref[:, HALF:], low[j])
            if j != 1:
                y = y + bias_ref[j // 2 : j // 2 + 1, cols]
            ref[:, cols] = y.astype(bf16)


def proj_kernel(x_ref, o_ref, w0, w1, w2, w3, vec_ref, h_ref, a_ref):
    def body(rows):
        o0, o1 = o_ref[rows, :HALF], o_ref[rows, HALF:]
        y = jnp.concatenate(
            [dot(o0, w0[...]) + dot(o1, w1[...]), dot(o0, w2[...]) + dot(o1, w3[...])], axis=1
        )
        h = x_ref[rows].astype(f32) + y + vec_ref[BIAS_PROJ : BIAS_PROJ + 1]
        hat, _ = standardize(h)
        h_ref[rows] = h
        a_ref[rows] = (
            hat * vec_ref[GAIN2 : GAIN2 + 1] + vec_ref[SHIFT2 : SHIFT2 + 1]
        ).astype(bf16)

    chunked(x_ref.shape[0], body)


def mlp_kernel(*refs):
    down_bit = refs[0]
    refs = refs[1:]
    side_ref, a_ref, dz_ref, h_ref, bias_ref, vec_ref = refs[:6]
    u, w = refs[6:12], refs[12:18]
    out_ref, da_ref, send2_ref, keep2_ref, send1_ref, keep1_ref, bsum_ref = refs[18:25]
    acc_ref, at_ref = refs[25:]
    hidden = u[0].shape[1]
    near = hidden // HALF // 2
    at_ref[...] = a_ref[...].T
    acc_ref[...] = h_ref[...] + vec_ref[BIAS_FC2 : BIAS_FC2 + 1]
    da_ref[...] = jnp.zeros_like(da_ref)
    z0, z1 = dz_ref[:, :HALF], dz_ref[:, HALF:]

    for side, grad2, grad1 in ((1, send2_ref, send1_ref), (0, keep2_ref, keep1_ref)):
        for half in range(2):
            up, down = u[2 + 2 * side + half], w[2 + 2 * side + half]
            down_else = w[2 + 2 * side + 1 - half]
            first = (side_ref[0, 0] if half == 0 else 1 - side_ref[0, 0]) * near
            same = side_ref[0, 0] == side_ref[down_bit, 0]

            @pl.loop(0, near)
            def _(
                t,
                side=side,
                grad2=grad2,
                grad1=grad1,
                up=up,
                down=down,
                down_else=down_else,
                first=first,
                same=same,
            ):
                here = pl.ds(pl.multiple_of(t * HALF, HALF), HALF)
                tile = pl.ds(pl.multiple_of((first + t) * HALF, HALF), HALF)
                where = pl.ds(pl.multiple_of(side * hidden + (first + t) * HALF, HALF), HALF)
                p0, p1 = u[side][:, tile], up[:, here]
                d0, d1 = w[side][tile], jnp.where(same, down[here], down_else[here])
                f = dot(a_ref[:, :HALF], p0) + dot(a_ref[:, HALF:], p1) + bias_ref[:, where]
                dm = dot_nt(z0, d0) + dot_nt(z1, d1)
                cdf = 0.5 * (1.0 + lax.erf(f * (0.5**0.5)))
                m = (f * cdf).astype(bf16)
                slope = cdf + f * (jnp.exp(-0.5 * f * f) * 0.3989422804014327)
                df = (dm * slope).astype(bf16)
                bsum_ref[:, where] = jnp.sum(df.astype(f32), axis=0, keepdims=True)
                acc_ref[:, :HALF] += dot(m, d0)
                acc_ref[:, HALF:] += dot(m, d1)
                da_ref[:, :HALF] += dot_nt(df, p0)
                da_ref[:, HALF:] += dot_nt(df, p1)
                mt = m.T
                grad2[0, tile] = dot(mt, z0).astype(bf16)
                grad2[1, tile] = dot(mt, z1).astype(bf16)
                grad1[0, tile] = dot(at_ref[:HALF], df).astype(bf16)
                grad1[1, tile] = dot(at_ref[HALF:], df).astype(bf16)

    out_ref[...] = acc_ref[...].astype(bf16)


def mid_kernel(
    da_ref, h_ref, dz_ref, o_ref, w0, w1, w2, w3, vec_ref, dh_ref, do_ref, send_ref, keep_ref, sum_ref, dy_ref
):
    sum_ref[...] = jnp.zeros_like(sum_ref)

    def body(rows):
        hat, scaling = standardize(h_ref[rows])
        da = da_ref[rows]
        dz = dz_ref[rows].astype(f32)
        du = standardize_back(da, hat, scaling, vec_ref[GAIN2 : GAIN2 + 1])
        dh = dz + du
        dh_ref[rows] = dh
        dy = dh.astype(bf16)
        dy_ref[rows] = dy
        y0, y1 = dy[:, :HALF], dy[:, HALF:]
        do_ref[rows] = jnp.concatenate(
            [dot_nt(y0, w0[...]) + dot_nt(y1, w2[...]), dot_nt(y0, w1[...]) + dot_nt(y1, w3[...])],
            axis=1,
        ).astype(bf16)
        add_sum(sum_ref, 0, da * hat)
        add_sum(sum_ref, 1, da)
        add_sum(sum_ref, 2, dy.astype(f32))
        add_sum(sum_ref, 3, dz)

    chunked(h_ref.shape[0], body)
    ot = o_ref[...].T
    for side, ref in enumerate((keep_ref, send_ref)):
        for c in range(2):
            ref[c] = dot(
                ot[side * HALF : (side + 1) * HALF], dy_ref[:, c * HALF : (c + 1) * HALF]
            ).astype(bf16)


def qkv_grad_kernel(a_ref, dq_ref, dk_ref, dv_ref, sendp_ref, keepp_ref, send_ref, keep_ref, sum_ref):
    at = a_ref[...].T
    for side, (ref, proj_ref) in enumerate(((keep_ref, keepp_ref), (send_ref, sendp_ref))):
        cols = slice(side * HALF, (side + 1) * HALF)
        ref[:, 3 * HALF :] = proj_ref[...]
        for j, d_ref in enumerate((dq_ref, dk_ref, dv_ref)):
            d = d_ref[:, cols]
            for c in range(2):
                ref[c, j * HALF : (j + 1) * HALF] = dot(at[c * HALF : (c + 1) * HALF], d).astype(bf16)
            if j != 1:
                sum_ref[j // 2 : j // 2 + 1, cols] = jnp.sum(d.astype(f32), axis=0, keepdims=True)


def leave_kernel(
    dq_ref, dk_ref, dv_ref, dh_ref, x_ref, w0, w1, w2, w3, vec_ref, order_ref, own_ref, other_ref, sum_ref, g_ref
):
    sum_ref[...] = jnp.zeros_like(sum_ref)

    def body(rows):
        da = []
        for top, low in ((w0, w1), (w2, w3)):
            part = None
            for j, ref in enumerate((dq_ref, dk_ref, dv_ref)):
                y = dot_nt(ref[rows, :HALF], top[j]) + dot_nt(ref[rows, HALF:], low[j])
                part = y if part is None else part + y
            da.append(part)
        da = jnp.concatenate(da, axis=1)
        hat, scaling = standardize(x_ref[rows].astype(f32))
        du = standardize_back(da, hat, scaling, vec_ref[GAIN1 : GAIN1 + 1])
        g_ref[rows] = (dh_ref[rows] + du).astype(bf16)
        add_sum(sum_ref, 0, da * hat)
        add_sum(sum_ref, 1, da)

    chunked(x_ref.shape[0], body)
    restore(g_ref, order_ref, own_ref, other_ref)


def restore(rows_ref, order_ref, own_ref, other_ref):
    images = own_ref.shape[0] // IMAGE
    for n in range(images):
        g = dot_tn(order_ref[...], rows_ref[n * 2 * PAIR : (n + 1) * 2 * PAIR])
        out = slice(n * IMAGE, (n + 1) * IMAGE)
        own_ref[out] = g[:, :HALF].astype(bf16)
        other_ref[out] = g[:, HALF:].astype(bf16)


def restore_kernel(rows_ref, order_ref, own_ref, other_ref):
    restore(rows_ref, order_ref, own_ref, other_ref)


def arrange_kernel(own_ref, other_ref, order_ref, out_ref):
    images = own_ref.shape[0] // IMAGE
    for n in range(images):
        rows = slice(n * IMAGE, (n + 1) * IMAGE)
        tok = jnp.concatenate([own_ref[rows], other_ref[rows]], axis=1)
        out_ref[n * 2 * PAIR : (n + 1) * 2 * PAIR] = dot(order_ref[...], tok).astype(bf16)


def row_add_kernel(keep_ref, got_ref, own_ref, away_ref):
    own_ref[...] = keep_ref[0] + got_ref[0]
    away_ref[...] = keep_ref[1] + got_ref[1]


def halve_kernel(bit, side_ref, own_ref, got_ref, mine_ref, away_ref):
    half = mine_ref.shape[-2]
    lead = (slice(None),) * (len(mine_ref.shape) - 2)
    for out_ref, at in ((mine_ref, side_ref[bit, 0]), (away_ref, 1 - side_ref[bit, 0])):
        rows = (*lead, pl.ds(pl.multiple_of(at * half, half), half))
        out_ref[...] = own_ref[rows] + got_ref[rows]


def add_kernel(own_ref, got_ref, out_ref):
    out_ref[...] = own_ref[...] + got_ref[...]


def double_kernel(bit, side_ref, own_ref, got_ref, out_ref):
    half = own_ref.shape[0]
    for ref, at in ((own_ref, side_ref[bit, 0]), (got_ref, 1 - side_ref[bit, 0])):
        out_ref[pl.ds(pl.multiple_of(at * half, half), half)] = ref[...]


def last_fc2_kernel(side_ref, own_ref, got_ref, out_ref):
    half = own_ref.shape[0]
    for ref, at in ((own_ref, side_ref[0, 0]), (got_ref, 1 - side_ref[0, 0])):
        out_ref[pl.ds(pl.multiple_of(at * half, half), half)] = ref[...].astype(f32)


def last_fc1_kernel(side_ref, own_ref, got_ref, out_ref):
    tiles = own_ref.shape[0] // HALF
    for ref, at in ((own_ref, side_ref[0, 0]), (got_ref, 1 - side_ref[0, 0])):
        for t in range(tiles):
            lanes = pl.ds(pl.multiple_of((at * tiles + t) * HALF, HALF), HALF)
            out_ref[:, lanes] = ref[t * HALF : (t + 1) * HALF].astype(f32)


def last_qkv_kernel(side_ref, own_ref, got_ref, qkv_ref, proj_ref):
    def place(low, high):
        qkv_ref[0] = low[:HALF].astype(f32)
        qkv_ref[1] = low[HALF:].astype(f32)
        qkv_ref[2] = high[:HALF].astype(f32)
        proj_ref[...] = high[HALF:].astype(f32)

    @pl.when(side_ref[0, 0] == 0)
    def _():
        place(own_ref, got_ref)

    @pl.when(side_ref[0, 0] != 0)
    def _():
        place(got_ref, own_ref)


SPLIT, FEATURES = 14, 6


def pack_kernel(qkv_ref, fc1_ref, table_ref, one_ref, two_ref, send_ref, keep_ref):
    for side, ref in enumerate((keep_ref, send_ref)):
        cols = slice(side * HALF, (side + 1) * HALF)
        ref[...] = jnp.zeros_like(ref)
        ref[0:2] = qkv_ref[:, cols]
        for t in range(4):
            at = (side * 4 + t) * HALF
            ref[2 + t : 3 + t] = fc1_ref[:, at : at + HALF]
        ref[6:SPLIT] = table_ref[side * 8 : side * 8 + 8]
        for c in range(2):
            at, half = SPLIT + c * FEATURES, slice(c * HALF, (c + 1) * HALF)
            ref[at : at + 2] = one_ref[:, half]
            ref[at + 2 : at + 6] = two_ref[:, half]


def small_row_kernel(keep_ref, got_ref, own_ref, away_ref):
    total = keep_ref[...] + got_ref[...]
    end = SPLIT + FEATURES
    for ref, at in ((own_ref, SPLIT), (away_ref, end)):
        ref[...] = jnp.zeros_like(ref)
        ref[:SPLIT] = total[:SPLIT]
        ref[SPLIT:end] = total[at : at + FEATURES]


def unpack_kernel(own_ref, got_ref, qkv_ref, fc1_ref, table_ref, gain_ref, shift_ref, proj_ref, fc2_ref):
    total = own_ref[...] + got_ref[...]
    qkv_ref[...] = total[0:2]
    for t in range(4):
        fc1_ref[:, t * HALF : (t + 1) * HALF] = total[2 + t : 3 + t]
    table_ref[...] = total[6:SPLIT].T[: table_ref.shape[0]]
    for j in range(2):
        gain_ref[j : j + 1] = total[SPLIT + 2 * j : SPLIT + 2 * j + 1]
        shift_ref[j : j + 1] = total[SPLIT + 2 * j + 1 : SPLIT + 2 * j + 2]
    proj_ref[...] = total[SPLIT + 4 : SPLIT + 5]
    fc2_ref[...] = total[SPLIT + 5 : SPLIT + 6]


def call(kernel, args, outs, scratch=(), flops=10**9, vmem=4):
    space = pl.BlockSpec(memory_space=pltpu.VMEM)
    return pl.pallas_call(
        kernel,
        in_specs=[space] * len(args),
        out_specs=[space] * len(outs),
        out_shape=[jax.ShapeDtypeStruct(shape, dtype) for shape, dtype in outs],
        scratch_shapes=[pltpu.VMEM(shape, dtype) for shape, dtype in scratch],
        cost_estimate=pl.CostEstimate(flops=flops, bytes_accessed=4 * 10**6, transcendentals=0),
        compiler_params=pltpu.CompilerParams(vmem_limit_bytes=vmem << 20),
    )(*args)


def both_cols(vector):
    return jnp.concatenate([vector, swap_col(vector)], axis=-1)


def both_rows(vector):
    return jnp.concatenate([vector, swap_row(vector)], axis=-1)


def gather_weight(weight):
    mine = swap_row(weight)
    other = swap_col(weight)
    return weight, mine, other, swap_row(other)


def relay_weight(half, bit):
    near = swap_col(half)
    far = swap(near, "dp", bit)
    near_row = swap_row(near)
    far_row = swap_row(far)
    return near, far, near_row, far_row


def swap_mixed(values, flip):
    dp, row, col = (lax.axis_size(name) for name in ("dp", "row", "col"))
    pairs = []
    for i in range(dp * row * col):
        c, r, d = i % col, i // col % row, i // (col * row)
        if r == flip:
            c = c ^ 1
        else:
            d = d ^ 1
        pairs.append((i, (d * row + r) * col + c))
    return lax.ppermute(values, ("dp", "row", "col"), pairs)


def mixed_first_kernel(side_ref, keep_ref, got_ref, own_ref, away_ref):
    half = own_ref.shape[0] // 2
    r, s = side_ref[ROW_FLAG, 0], side_ref[0, 0]

    def put(ref, at, c, x):
        rows = pl.ds(pl.multiple_of(x * half, half), half)
        ref[at * half : (at + 1) * half] = keep_ref[c, rows] + got_ref[c, rows]

    put(own_ref, 0, 0, r * s)
    put(own_ref, 1, r, 1 - r * (1 - s))
    put(away_ref, 0, 1 - r, r * (1 - s))
    put(away_ref, 1, 1, 1 - r * s)


def mixed_second_kernel(side_ref, own_ref, got_ref, mine_ref, away_ref):
    half = mine_ref.shape[0]
    at = (1 - side_ref[ROW_FLAG, 0]) * side_ref[0, 0]
    for ref, where in ((mine_ref, at), (away_ref, 1 - at)):
        rows = pl.ds(pl.multiple_of(where * half, half), half)
        ref[...] = own_ref[rows] + got_ref[rows]


def reduce_weight(send, keep, sides, way, last, outs):
    bits = lax.axis_size("dp").bit_length() - 1
    halved = bits - 1
    small = 10**8

    def halve(own, got, bit):
        shape = own.shape[:-2] + (own.shape[-2] // 2, own.shape[-1])
        own, away = call(
            functools.partial(halve_kernel, bit),
            (sides, own, got),
            [(shape, bf16)] * 2,
            flops=small,
        )
        return own, swap(away, "dp", bit)

    got = swap_row(send)
    own, start = keep, 0
    if way == "m":
        shape = own.shape[1:]
        own, away = call(mixed_first_kernel, (sides, own, got), [(shape, bf16)] * 2, flops=small)
        got = swap_mixed(away, 0)
        shape = (shape[0] // 2, shape[1])
        own, away = call(mixed_second_kernel, (sides, own, got), [(shape, bf16)] * 2, flops=small)
        got = swap_mixed(away, 1)
        start = 1
    else:
        if way == "x":
            own, got = halve(own, got, 0)
            start = 1
        own, away = call(row_add_kernel, (own, got), [(own.shape[1:], bf16)] * 2, flops=small)
        got = swap_col(away)
    for bit in range(start, halved):
        own, got = halve(own, got, bit)
    for bit in (bits - 1,):
        (own,) = call(add_kernel, (own, got), [(own.shape, bf16)], flops=small)
        got = swap(own, "dp", bit)
    (own,) = call(add_kernel, (own, got), [(own.shape, bf16)], flops=small)
    for bit in reversed(range(halved)):
        got = swap(own, "dp", bit)
        if bit:
            (own,) = call(
                functools.partial(double_kernel, bit),
                (sides, own, got),
                [((2 * own.shape[0], own.shape[1]), bf16)],
                flops=small,
            )
    return call(last, (sides, own, got), outs, flops=small)


def shards(
    tokens,
    qkv_weight,
    qkv_bias,
    pos_table,
    rel_index,
    region_ids,
    shifts,
    proj_weight,
    proj_bias,
    layer_norm_scales,
    layer_norm_biases,
    fc1_weight,
    fc1_bias,
    fc2_weight,
    fc2_bias,
    cotangent,
):
    col = lax.axis_index("col")
    me = lax.axis_index("dp")
    bits = lax.axis_size("dp").bit_length() - 1
    rows = tokens.shape[0] // 2
    down_bit = 1 if bits > 1 else 0

    def exchange(keep, send):
        return keep, swap_col(send)

    def split(values):
        keep = lax.dynamic_slice_in_dim(values, col * rows, rows, 0)
        return keep, lax.dynamic_slice_in_dim(values, (1 - col) * rows, rows, 0)

    def give_back(keep, send, dtype):
        other = swap_col(send)
        keep, other = keep.astype(dtype), other.astype(dtype)
        return jnp.where(
            col == 0,
            jnp.concatenate([keep, other], axis=0),
            jnp.concatenate([other, keep], axis=0),
        )

    def halved(weight, dim, bit):
        size = weight.shape[dim] // 2
        return lax.dynamic_slice_in_dim(weight, ((me >> bit) & 1) * size, size, dim)

    def with_row(weight):
        return weight, swap_row(weight)

    wfc1 = (*with_row(fc1_weight), *relay_weight(halved(fc1_weight, 1, 0), 0))
    wfc2 = (*with_row(fc2_weight), *relay_weight(halved(fc2_weight, 0, down_bit), down_bit))
    vectors = both_cols(
        jnp.stack(
            [
                layer_norm_scales[0],
                layer_norm_scales[1],
                layer_norm_biases[0],
                layer_norm_biases[1],
                proj_bias,
                fc2_bias,
            ]
        ),
    )
    bias_fc1 = both_rows(fc1_bias)
    bias_qkv = both_rows(qkv_bias)
    table = both_rows(pos_table)
    entries, heads = table.shape
    row_bit = lax.axis_index("row")
    flags = [(me >> bit) & 1 for bit in range(min(bits, ROW_FLAG))]
    flags += [jnp.int32(0)] * (ROW_FLAG - len(flags)) + [row_bit]
    sides_in = jnp.broadcast_to(jnp.stack(flags).astype(jnp.int32)[:, None], (ROW_FLAG + 1, 128))

    place = jnp.arange(2 * PAIR, dtype=jnp.int32)
    pair, inside = place // PAIR, place % PAIR
    window = 2 * pair + inside // CELLS
    spot = inside % CELLS
    cell_i = (window // 2) * WIN + spot // WIN
    cell_j = (window % 2) * WIN + spot % WIN
    token = ((cell_i + shifts[0]) % SIDE) * SIDE + (cell_j + shifts[1]) % SIDE
    token = jnp.where(inside < 2 * CELLS, token, -1)
    order = (token[:, None] == jnp.arange(IMAGE, dtype=jnp.int32)[None, :]).astype(bf16)

    index_t = rel_index.T
    lookup = (index_t.reshape(-1)[:, None] == jnp.arange(entries)[None, :]).astype(f32)
    pos = jnp.dot(lookup, table, precision=highest).T.reshape(heads, CELLS, CELLS)
    per_side = SIDE // WIN
    zones = region_ids.reshape(per_side, WIN, per_side, WIN).transpose(0, 2, 1, 3)
    zones = zones.reshape(per_side * per_side, CELLS)
    allowed = zones[:, :, None] == zones[:, None, :]
    biased = jnp.where(allowed[:, None], pos[None], masked_value)

    def corner(values, low, fill):
        high = PAIR - low - CELLS
        pad = [(0, 0)] * (values.ndim - 2) + [(low, high), (low, high + 128 - PAIR)]
        return jnp.pad(values, pad, constant_values=fill)

    bias = jnp.maximum(
        corner(biased[0::2], 0, masked_value), corner(biased[1::2], CELLS, masked_value)
    )
    pair_index = jnp.maximum(corner(index_t, 0, -1), corner(index_t, CELLS, -1))

    x_own, x_other = exchange(*split(tokens))
    qkv_blocks, bias, pair_index, sides_in, order = lax.optimization_barrier(
        (qkv_weight.transpose(1, 0, 2), bias, pair_index, sides_in, order)
    )
    wqkv = gather_weight(qkv_blocks)
    wproj = gather_weight(proj_weight)
    z_own, z_other = exchange(*split(cotangent))

    count = rows // IMAGE * 2 * PAIR
    width = 2 * tokens.shape[1]
    wide = (count, width)
    x, a1, sides = call(
        enter_kernel,
        (sides_in, x_own, x_other, order, vectors),
        [(wide, bf16), (wide, bf16), (sides_in.shape, jnp.int32)],
    )
    q, k, v = call(qkv_kernel, (a1, *wqkv, bias_qkv), [(wide, bf16)] * 3)
    probs, o = call(
        attend_kernel,
        (q, k, v, bias),
        [((count // PAIR, heads, PAIR, 128), bf16), (wide, bf16)],
        vmem=8,
    )
    h1, a2 = call(proj_kernel, (x, o, *wproj, vectors), [(wide, f32), (wide, bf16)])
    (dz,) = call(arrange_kernel, (z_own, z_other, order), [(wide, bf16)])
    block = ((2, 4 * HALF, HALF), bf16)
    out_rows, da2, send2, keep2, send1, keep1, df_sum = call(
        functools.partial(mlp_kernel, down_bit),
        (sides, a2, dz, h1, bias_fc1[None], vectors, *wfc1, *wfc2),
        [
            (wide, bf16),
            (wide, f32),
            block,
            block,
            block,
            block,
            ((1, bias_fc1.shape[0]), f32),
        ],
        scratch=[(wide, f32), (wide[::-1], bf16)],
        flops=3 * 10**9,
        vmem=8,
    )
    (fc2_grad,) = reduce_weight(
        send2, keep2, sides, "m", last_fc2_kernel, [(fc2_weight.shape, f32)]
    )
    (fc1_grad,) = reduce_weight(
        send1, keep1, sides, "m", last_fc1_kernel, [(fc1_weight.shape, f32)]
    )
    half = (rows, tokens.shape[1])
    out_own, out_other = call(restore_kernel, (out_rows, order), [(half, bf16)] * 2)
    out = give_back(out_own, out_other, bf16)

    blockp = ((2, *proj_weight.shape), bf16)
    dh1, do, sendp, keepp, sums_two = call(
        mid_kernel,
        (da2, h1, dz, o, *wproj, vectors),
        [(wide, f32), (wide, bf16), blockp, blockp, ((4, width), f32)],
        scratch=[(wide, bf16)],
    )
    dq, dk, dv, ds = call(
        attend_back_kernel,
        (q, k, v, probs, do),
        [(wide, bf16)] * 3 + [((heads, PAIR, 128), f32)],
        vmem=8,
    )
    sendq, keepq, sums_qkv = call(
        qkv_grad_kernel, (a1, dq, dk, dv, sendp, keepp), [block, block, ((2, width), f32)]
    )
    qkv_grad, proj_grad = reduce_weight(
        sendq,
        keepq,
        sides,
        "m",
        last_qkv_kernel,
        [((3, HALF, HALF), f32), (proj_weight.shape, f32)],
    )
    g_own, g_other, sums_one = call(
        leave_kernel,
        (dq, dk, dv, dh1, x, *wqkv, vectors, order),
        [(half, bf16), (half, bf16), ((2, width), f32)],
        scratch=[(wide, bf16)],
    )
    grad_input = give_back(g_own, g_other, f32)

    (table_sums,) = call(table_kernel, (ds, pair_index), [((heads, HALF), f32)])
    small = ((32, HALF), f32)
    sent, own = call(pack_kernel, (sums_qkv, df_sum, table_sums, sums_one, sums_two), [small] * 2)
    got = swap_row(sent)
    small = ((24, HALF), f32)
    own, away = call(small_row_kernel, (own, got), [small] * 2)
    got = swap_col(away)
    for bit in range(bits):
        (own,) = call(add_kernel, (own, got), [small])
        got = swap(own, "dp", bit)
    qkv_bias_grad, fc1_bias_grad, table_grad, gains, shifted, proj_bias_grad, fc2_bias_grad = call(
        unpack_kernel,
        (own, got),
        [
            ((2, HALF), f32),
            ((1, fc1_bias.shape[0]), f32),
            (pos_table.shape, f32),
            ((2, HALF), f32),
            ((2, HALF), f32),
            ((1, HALF), f32),
            ((1, HALF), f32),
        ],
    )
    return (
        out,
        grad_input,
        qkv_grad.transpose(1, 0, 2),
        qkv_bias_grad,
        table_grad,
        proj_grad,
        proj_bias_grad[0],
        gains,
        shifted,
        fc1_grad,
        fc1_bias_grad[0],
        fc2_grad,
        fc2_bias_grad[0],
    )


def solution(mesh):
    return jax.shard_map(
        shards,
        mesh=mesh,
        in_specs=(
            P(("dp", "row"), "col"),
            P("col", None, "row"),
            P(None, "row"),
            P(None, "row"),
            P(),
            P(),
            P(),
            P("row", "col"),
            P("col"),
            P(None, "col"),
            P(None, "col"),
            P("col", "row"),
            P("row"),
            P("row", "col"),
            P("col"),
            P(("dp", "row"), "col"),
        ),
        out_specs=(
            P(("dp", "row"), "col"),
            P(("dp", "row"), "col"),
            P("col", None, "row"),
            P(None, "row"),
            P(None, "row"),
            P("row", "col"),
            P("col"),
            P(None, "col"),
            P(None, "col"),
            P("col", "row"),
            P("row"),
            P("row", "col"),
            P("col"),
        ),
        check_vma=False,
    )
```

```python
import functools

import jax
import jax.numpy as jnp
from jax import lax
from jax.experimental import pallas as pl
from jax.experimental.pallas import tpu as pltpu
from jax.sharding import PartitionSpec as P


HEAD_DIM = 32
WIN = 7
SIDE = 14
CELLS = WIN * WIN
IMAGE = SIDE * SIDE
PAIR = 112
GROUP = 128 // HEAD_DIM

highest = lax.Precision.HIGHEST
epsilon = 1e-05
masked_value = -1000000000.0
score_scale = HEAD_DIM ** (-0.5)
f32 = jnp.float32
bf16 = jnp.bfloat16


DP, ROW, COL = "dp", "row", "col"


def swap(values, axis, bit=0):
    size = lax.axis_size(axis)
    return lax.ppermute(values, axis, [(i, i ^ (1 << bit)) for i in range(size)])


def swap_row(values):
    return swap(values, ROW)


def swap_col(values):
    return swap(values, COL)


def dot(a, b):
    return jnp.dot(a, b, preferred_element_type=f32)


def dot_nt(a, b):
    return lax.dot_general(a, b, (((1,), (1,)), ((), ())), preferred_element_type=f32)


def dot_tn(a, b):
    return lax.dot_general(a, b, (((0,), (0,)), ((), ())), preferred_element_type=f32)


def lane_group():
    return lax.broadcasted_iota(jnp.int32, (PAIR, 128), 1) // HEAD_DIM


def fill_lanes(rows):
    return jnp.concatenate([rows, jnp.zeros((128 - PAIR, 128), rows.dtype)], axis=0)


def stack_heads(rows, lanes):
    zero = jnp.zeros_like(rows)
    return jnp.concatenate([jnp.where(lanes == j, rows, zero) for j in range(GROUP)], axis=0)


def pick_heads(parts, lanes):
    total = parts[0]
    for j in range(1, GROUP):
        total = jnp.where(lanes == j, parts[j], total)
    return total


def attend_kernel(q_ref, k_ref, v_ref, bias_ref, p_ref, o_ref):
    lanes = lane_group()

    @pl.loop(0, q_ref.shape[0] // PAIR)
    def _(i):
        rows = pl.ds(pl.multiple_of(i * PAIR, PAIR), PAIR)
        for g in range(bias_ref.shape[1] // GROUP):
            cols = slice(g * 128, (g + 1) * 128)
            heads = slice(g * GROUP, (g + 1) * GROUP)
            v = v_ref[rows, cols]
            s = dot_nt(stack_heads(k_ref[rows, cols], lanes), fill_lanes(q_ref[rows, cols]))
            s = s.reshape(GROUP, PAIR, 128) * score_scale + bias_ref[lax.rem(i, 2), heads]
            e = jnp.exp(s - jnp.max(s, axis=1, keepdims=True))
            p = (e * (1.0 / jnp.sum(e, axis=1, keepdims=True))).astype(bf16)
            p_ref[i, heads] = p
            o_ref[rows, cols] = pick_heads(
                [dot_tn(p[j], v)[:PAIR] for j in range(GROUP)], lanes
            ).astype(bf16)


def attend_back_kernel(q_ref, k_ref, v_ref, p_ref, do_ref, dq_ref, dk_ref, dv_ref, ds_ref):
    lanes = lane_group()
    ds_ref[...] = jnp.zeros_like(ds_ref)

    @pl.loop(0, q_ref.shape[0] // PAIR)
    def _(i):
        rows = pl.ds(pl.multiple_of(i * PAIR, PAIR), PAIR)
        for g in range(p_ref.shape[1] // GROUP):
            cols = slice(g * 128, (g + 1) * 128)
            heads = slice(g * GROUP, (g + 1) * GROUP)
            k = k_ref[rows, cols]
            q = fill_lanes(q_ref[rows, cols])
            do = fill_lanes(do_ref[rows, cols])
            p = p_ref[i, heads]
            pf = p.astype(f32)
            dp = dot_nt(stack_heads(v_ref[rows, cols], lanes), do).reshape(GROUP, PAIR, 128)
            ds = (pf * (dp - jnp.sum(pf * dp, axis=1, keepdims=True))).astype(bf16)
            ds_ref[heads] += ds.astype(f32)
            dk = dot(ds.reshape(GROUP * PAIR, 128), q).reshape(GROUP, PAIR, 128)
            dv = dot(p.reshape(GROUP * PAIR, 128), do).reshape(GROUP, PAIR, 128)
            dq = [dot_tn(ds[j], k)[:PAIR] for j in range(GROUP)]
            dq_ref[rows, cols] = (pick_heads(dq, lanes) * score_scale).astype(bf16)
            dk_ref[rows, cols] = (pick_heads(dk, lanes) * score_scale).astype(bf16)
            dv_ref[rows, cols] = pick_heads(dv, lanes).astype(bf16)


def table_kernel(ds_ref, index_ref, out_ref):
    entries = lax.broadcasted_iota(jnp.int32, (HALF, 128), 0).astype(f32).astype(bf16)
    one_hit, no_hit = jnp.ones((HALF, 128), bf16), jnp.zeros((HALF, 128), bf16)
    heads = ds_ref.shape[0]
    out_ref[...] = jnp.zeros_like(out_ref)

    @pl.loop(0, CELLS // WIN)
    def _(step):
        base = step * 2 * WIN
        total = jnp.zeros((2 * heads, HALF), f32)
        for pair in range(WIN):
            parts, hits = [], []
            for one in range(2):
                at = pl.ds(base + 2 * pair + one, 1)
                ds = ds_ref[:, at, :].reshape(heads, 128)
                high = ds.astype(bf16)
                low = (ds - high.astype(f32)).astype(bf16)
                parts.append(jnp.concatenate([high, low], axis=0))
                hits.append(jnp.where(entries == index_ref[at, :].astype(bf16), one_hit, no_hit))
            total = total + dot_nt(jnp.concatenate(parts, axis=1), jnp.concatenate(hits, axis=1))
        out_ref[...] += total[:heads] + total[heads:]


def chunked(rows, body):
    @pl.loop(0, rows // PAIR)
    def _(i):
        body(pl.ds(pl.multiple_of(i * PAIR, PAIR), PAIR))


def standardize(values):
    center = jnp.mean(values, axis=1, keepdims=True)
    centered = values - center
    scaling = lax.rsqrt(jnp.mean(centered * centered, axis=1, keepdims=True) + epsilon)
    return centered * scaling, scaling


def standardize_back(grad, hat, scaling, gain):
    scaled = grad * gain
    first = jnp.mean(scaled, axis=1, keepdims=True)
    second = jnp.mean(scaled * hat, axis=1, keepdims=True)
    return scaling * (scaled - first - hat * second)


def add_sum(ref, row, values):
    ref[row : row + 1, :] += jnp.sum(values, axis=0, keepdims=True)


ROW_FLAG, COL_FLAG, SHIFT_FLAG = 4, 5, 6
GAIN1, GAIN2, SHIFT1, SHIFT2, BIAS_PROJ, BIAS_FC2 = range(6)
HALF = 256


def window_order(shift_i, shift_j):
    place = lax.broadcasted_iota(jnp.int32, (2 * PAIR, 1), 0)
    pair = (place >= PAIR).astype(jnp.int32)
    inside = place - PAIR * pair
    right = (inside >= CELLS).astype(jnp.int32)
    spot = inside - CELLS * right
    down = (spot * 37) >> 8
    i = pair * WIN + down + shift_i
    j = right * WIN + spot - WIN * down + shift_j
    i = jnp.where(i >= SIDE, i - SIDE, i)
    j = jnp.where(j >= SIDE, j - SIDE, j)
    token = jnp.where(inside < 2 * CELLS, i * SIDE + j, -1)
    hit = token == lax.broadcasted_iota(jnp.int32, (2 * PAIR, IMAGE), 1)
    return hit.astype(f32).astype(bf16)


def my_half(ref, at):
    rows = ref.shape[0] // 2
    return ref[pl.ds(pl.multiple_of(at * rows, 8), rows)]


def enter_kernel(side_in, own_ref, other_ref, vec_ref, x_ref, a_ref, order_ref, side_ref):
    side_ref[...] = side_in[...]
    order_ref[...] = window_order(side_in[SHIFT_FLAG, 0], side_in[SHIFT_FLAG + 1, 0])
    images = other_ref.shape[0] // IMAGE
    own = my_half(own_ref, side_in[COL_FLAG, 0])
    for n in range(images):
        rows = slice(n * IMAGE, (n + 1) * IMAGE)
        tok = jnp.concatenate([own[rows], other_ref[rows]], axis=1)
        x = dot(order_ref[...], tok)
        hat, _ = standardize(x)
        a = hat * vec_ref[GAIN1 : GAIN1 + 1] + vec_ref[SHIFT1 : SHIFT1 + 1]
        out = slice(n * 2 * PAIR, (n + 1) * 2 * PAIR)
        x_ref[out] = x.astype(bf16)
        a_ref[out] = a.astype(bf16)


def qkv_kernel(side_ref, a_ref, w0, w1, n2, f2, n3, f3, bias_ref, q_ref, k_ref, v_ref):
    s = side_ref[0, 0]
    near = a_ref[:, pl.ds(pl.multiple_of(HALF + s * 128, 128), 128)]
    far = a_ref[:, pl.ds(pl.multiple_of(HALF + (1 - s) * 128, 128), 128)]
    for side, (top, low0, low1) in enumerate(((w0, n2, f2), (w1, n3, f3))):
        cols = slice(side * HALF, (side + 1) * HALF)
        for j, ref in enumerate((q_ref, k_ref, v_ref)):
            y = dot(a_ref[:, :HALF], top[j]) + dot(near, low0[j]) + dot(far, low1[j])
            if j != 1:
                y = y + bias_ref[j // 2 : j // 2 + 1, cols]
            ref[:, cols] = y.astype(bf16)


def proj_kernel(x_ref, o_ref, w0, w1, w2, w3, vec_ref, h_ref, a_ref):
    def body(rows):
        o0, o1 = o_ref[rows, :HALF], o_ref[rows, HALF:]
        y = jnp.concatenate(
            [dot(o0, w0[...]) + dot(o1, w1[...]), dot(o0, w2[...]) + dot(o1, w3[...])], axis=1
        )
        h = x_ref[rows].astype(f32) + y + vec_ref[BIAS_PROJ : BIAS_PROJ + 1]
        hat, _ = standardize(h)
        h_ref[rows] = h
        a_ref[rows] = (
            hat * vec_ref[GAIN2 : GAIN2 + 1] + vec_ref[SHIFT2 : SHIFT2 + 1]
        ).astype(bf16)

    chunked(x_ref.shape[0], body)


def mlp_kernel(side, down_bit, *refs):
    side_ref, a_ref, dz_ref, bias_ref, vec_ref = refs[:5]
    u, w = refs[5:8], refs[8:11]
    if side:
        h_ref = refs[11]
        acc_ref, da_ref, grad2_ref, grad1_ref, bsum_ref, at_ref = refs[12:]
        at_ref[...] = a_ref[...].T
        acc_ref[...] = h_ref[...] + vec_ref[BIAS_FC2 : BIAS_FC2 + 1]
        da_ref[...] = jnp.zeros_like(da_ref)
        acc_in, da_in = acc_ref, da_ref
    else:
        acc_in, da_in, at_ref = refs[11:14]
        out_ref, da_ref, grad2_ref, grad1_ref, bsum_ref, acc_ref = refs[14:]
        acc_ref[...] = acc_in[...]
        da_ref[...] = da_in[...]
    hidden = u[0].shape[1]
    near = hidden // HALF // 2
    z0, z1 = dz_ref[:, :HALF], dz_ref[:, HALF:]
    same = side_ref[0, 0] == side_ref[down_bit, 0]

    for half in range(2):
        up, down, down_else = u[1 + half], w[1 + half], w[2 - half]
        first = (side_ref[0, 0] if half == 0 else 1 - side_ref[0, 0]) * near

        @pl.loop(0, near)
        def _(t, up=up, down=down, down_else=down_else, first=first):
            here = pl.ds(pl.multiple_of(t * HALF, HALF), HALF)
            tile = pl.ds(pl.multiple_of((first + t) * HALF, HALF), HALF)
            p0, p1 = u[0][:, tile], up[:, here]
            d0, d1 = w[0][tile], jnp.where(same, down[here], down_else[here])
            f = dot(a_ref[:, :HALF], p0) + dot(a_ref[:, HALF:], p1) + bias_ref[:, tile]
            dm = dot_nt(z0, d0) + dot_nt(z1, d1)
            cdf = 0.5 * (1.0 + lax.erf(f * (0.5**0.5)))
            m = (f * cdf).astype(bf16)
            slope = cdf + f * (jnp.exp(-0.5 * f * f) * 0.3989422804014327)
            df = (dm * slope).astype(bf16)
            bsum_ref[:, tile] = jnp.sum(df.astype(f32), axis=0, keepdims=True)
            acc_ref[:, :HALF] += dot(m, d0)
            acc_ref[:, HALF:] += dot(m, d1)
            da_ref[:, :HALF] += dot_nt(df, p0)
            da_ref[:, HALF:] += dot_nt(df, p1)
            mt = m.T
            grad2_ref[0, tile] = dot(mt, z0).astype(bf16)
            grad2_ref[1, tile] = dot(mt, z1).astype(bf16)
            grad1_ref[0, tile] = dot(at_ref[:HALF], df).astype(bf16)
            grad1_ref[1, tile] = dot(at_ref[HALF:], df).astype(bf16)

    if not side:
        out_ref[...] = acc_ref[...].astype(bf16)


def mid_kernel(
    da_ref, h_ref, dz_ref, o_ref, w0, w1, w2, w3, vec_ref, dh_ref, do_ref, send_ref, keep_ref, sum_ref, dy_ref
):
    sum_ref[...] = jnp.zeros_like(sum_ref)

    def body(rows):
        hat, scaling = standardize(h_ref[rows])
        da = da_ref[rows]
        dz = dz_ref[rows].astype(f32)
        du = standardize_back(da, hat, scaling, vec_ref[GAIN2 : GAIN2 + 1])
        dh = dz + du
        dh_ref[rows] = dh
        dy = dh.astype(bf16)
        dy_ref[rows] = dy
        y0, y1 = dy[:, :HALF], dy[:, HALF:]
        do_ref[rows] = jnp.concatenate(
            [dot_nt(y0, w0[...]) + dot_nt(y1, w2[...]), dot_nt(y0, w1[...]) + dot_nt(y1, w3[...])],
            axis=1,
        ).astype(bf16)
        add_sum(sum_ref, 0, da * hat)
        add_sum(sum_ref, 1, da)
        add_sum(sum_ref, 2, dy.astype(f32))
        add_sum(sum_ref, 3, dz)

    chunked(h_ref.shape[0], body)
    ot = o_ref[...].T
    for side, ref in enumerate((keep_ref, send_ref)):
        for c in range(2):
            ref[c] = dot(
                ot[side * HALF : (side + 1) * HALF], dy_ref[:, c * HALF : (c + 1) * HALF]
            ).astype(bf16)


def qkv_grad_kernel(a_ref, dq_ref, dk_ref, dv_ref, sendp_ref, keepp_ref, send_ref, keep_ref, sum_ref):
    at = a_ref[...].T
    for side, (ref, proj_ref) in enumerate(((keep_ref, keepp_ref), (send_ref, sendp_ref))):
        cols = slice(side * HALF, (side + 1) * HALF)
        ref[:, 3 * HALF :] = proj_ref[...]
        for j, d_ref in enumerate((dq_ref, dk_ref, dv_ref)):
            d = d_ref[:, cols]
            for c in range(2):
                ref[c, j * HALF : (j + 1) * HALF] = dot(at[c * HALF : (c + 1) * HALF], d).astype(bf16)
            if j != 1:
                sum_ref[j // 2 : j // 2 + 1, cols] = jnp.sum(d.astype(f32), axis=0, keepdims=True)


def leave_kernel(
    side_ref,
    dq_ref,
    dk_ref,
    dv_ref,
    dh_ref,
    x_ref,
    w0,
    w1,
    n2,
    f2,
    n3,
    f3,
    vec_ref,
    order_ref,
    out_ref,
    own_ref,
    other_ref,
    sum_ref,
    g_ref,
):
    sum_ref[...] = jnp.zeros_like(sum_ref)
    even = side_ref[0, 0] == 0

    def body(rows):
        def part(mine, other):
            total = None
            for j, ref in enumerate((dq_ref, dk_ref, dv_ref)):
                y = dot_nt(ref[rows, :HALF], mine[j]) + dot_nt(ref[rows, HALF:], other[j])
                total = y if total is None else total + y
            return total

        near, far = part(n2, n3), part(f2, f3)
        da = jnp.concatenate(
            [part(w0, w1), jnp.where(even, near, far), jnp.where(even, far, near)], axis=1
        )
        hat, scaling = standardize(x_ref[rows].astype(f32))
        du = standardize_back(da, hat, scaling, vec_ref[GAIN1 : GAIN1 + 1])
        g_ref[rows] = (dh_ref[rows] + du).astype(bf16)
        add_sum(sum_ref, 0, da * hat)
        add_sum(sum_ref, 1, da)

    chunked(x_ref.shape[0], body)
    for j, rows_ref in enumerate((out_ref, g_ref)):
        for n in range(own_ref.shape[1] // IMAGE):
            g = dot_tn(order_ref[...], rows_ref[n * 2 * PAIR : (n + 1) * 2 * PAIR])
            at = slice(n * IMAGE, (n + 1) * IMAGE)
            own_ref[j, at] = g[:, :HALF].astype(bf16)
            other_ref[j, at] = g[:, HALF:].astype(bf16)


def finish_kernel(side_ref, own_ref, got_ref, out_ref, grad_ref):
    rows = own_ref.shape[1]
    at = side_ref[COL_FLAG, 0]
    for ref, place in ((own_ref, at), (got_ref, 1 - at)):
        where = pl.ds(pl.multiple_of(place * rows, 8), rows)
        out_ref[where] = ref[0]
        grad_ref[where] = ref[1].astype(f32)


def arrange_kernel(side_ref, own_ref, other_ref, order_ref, out_ref):
    images = other_ref.shape[0] // IMAGE
    own = my_half(own_ref, side_ref[COL_FLAG, 0])
    for n in range(images):
        rows = slice(n * IMAGE, (n + 1) * IMAGE)
        tok = jnp.concatenate([own[rows], other_ref[rows]], axis=1)
        out_ref[n * 2 * PAIR : (n + 1) * 2 * PAIR] = dot(order_ref[...], tok).astype(bf16)


def halve_both_kernel(bit, side_ref, keep_ref, got_ref, mine_ref, away_ref):
    half = mine_ref.shape[1]
    for ref, at in ((mine_ref, side_ref[bit, 0]), (away_ref, 1 - side_ref[bit, 0])):
        rows = pl.ds(pl.multiple_of(at * half, 16), half)
        ref[...] = keep_ref[:, rows] + got_ref[:, rows]


def halve_kernel(bit, side_ref, own_ref, got_ref, mine_ref, away_ref):
    half = mine_ref.shape[0]
    for ref, at in ((mine_ref, side_ref[bit, 0]), (away_ref, 1 - side_ref[bit, 0])):
        rows = pl.ds(pl.multiple_of(at * half, 16), half)
        ref[...] = own_ref[rows] + got_ref[rows]


def add_kernel(own_ref, got_ref, out_ref):
    out_ref[...] = own_ref[...] + got_ref[...]


def double_kernel(bit, side_ref, own_ref, got_ref, out_ref):
    half = own_ref.shape[0]
    for ref, at in ((own_ref, side_ref[bit, 0]), (got_ref, 1 - side_ref[bit, 0])):
        out_ref[pl.ds(pl.multiple_of(at * half, 16), half)] = ref[...]


def join_kernel(own_ref, got_ref, out_ref):
    out_ref[0] = own_ref[...]
    out_ref[1] = got_ref[...]


def quarters(z_first, side_ref, own_ref, got_ref):
    r, x, z = side_ref[ROW_FLAG, 0], side_ref[0, 0], side_ref[1, 0]

    def place(x, z):
        return 2 * z + x if z_first else 2 * x + z

    mixed_x, mixed_z = x + r * (1 - 2 * x), z + (1 - r) * (1 - 2 * z)
    return (
        (own_ref[0], place(x, z)),
        (own_ref[1], place(mixed_x, mixed_z)),
        (got_ref[0], place(1 - mixed_x, 1 - mixed_z)),
        (got_ref[1], place(1 - x, 1 - z)),
    )


def last_fc2_kernel(z_first, side_ref, own_ref, got_ref, out_ref):
    rows = own_ref.shape[1]
    for values, at in quarters(z_first, side_ref, own_ref, got_ref):
        out_ref[pl.ds(pl.multiple_of(at * rows, 16), rows)] = values.astype(f32)


def last_fc1_kernel(z_first, side_ref, own_ref, got_ref, out_ref):
    for values, at in quarters(z_first, side_ref, own_ref, got_ref):
        out_ref[:, pl.ds(pl.multiple_of(at * HALF, HALF), HALF)] = values.astype(f32)


def last_qkv_kernel(z_first, side_ref, own_ref, got_ref, qkv_ref, proj_ref):
    for values, at in quarters(z_first, side_ref, own_ref, got_ref):

        @pl.when(at == 3)
        def _(values=values):
            proj_ref[...] = values.astype(f32)

        @pl.when(at < 3)
        def _(values=values, at=at):
            qkv_ref[pl.ds(lax.min(at, 2), 1)] = values.astype(f32)[None]


SPLIT, FEATURES = 14, 6


def pack_kernel(qkv_ref, mine1_ref, other1_ref, table_ref, one_ref, two_ref, send_ref, keep_ref):
    for side, (ref, fc1_ref) in enumerate(((keep_ref, mine1_ref), (send_ref, other1_ref))):
        cols = slice(side * HALF, (side + 1) * HALF)
        ref[...] = jnp.zeros_like(ref)
        ref[0:2] = qkv_ref[:, cols]
        for t in range(4):
            ref[2 + t : 3 + t] = fc1_ref[:, t * HALF : (t + 1) * HALF]
        ref[6:SPLIT] = table_ref[side * 8 : side * 8 + 8]
        for c in range(2):
            at, half = SPLIT + c * FEATURES, slice(c * HALF, (c + 1) * HALF)
            ref[at : at + 2] = one_ref[:, half]
            ref[at + 2 : at + 6] = two_ref[:, half]


def split_kernel(keep_ref, got_ref, own_ref, away_ref):
    total = keep_ref[...] + got_ref[...]
    end = SPLIT + FEATURES
    for ref, at in ((own_ref, SPLIT), (away_ref, end)):
        ref[...] = jnp.zeros_like(ref)
        ref[:SPLIT] = total[:SPLIT]
        ref[SPLIT:end] = total[at : at + FEATURES]


def unpack_kernel(own_ref, got_ref, bq_ref, b1_ref, table_ref, gain_ref, shift_ref, bp_ref, b2_ref):
    total = own_ref[...] + got_ref[...]
    bq_ref[...] = total[0:2]
    for t in range(4):
        b1_ref[:, t * HALF : (t + 1) * HALF] = total[2 + t : 3 + t]
    table_ref[...] = total[6:SPLIT, : table_ref.shape[1]]
    for j in range(2):
        gain_ref[j : j + 1] = total[SPLIT + 2 * j : SPLIT + 2 * j + 1]
        shift_ref[j : j + 1] = total[SPLIT + 2 * j + 1 : SPLIT + 2 * j + 2]
    bp_ref[...] = total[SPLIT + 4 : SPLIT + 5]
    b2_ref[...] = total[SPLIT + 5 : SPLIT + 6]


def call(kernel, args, outs, scratch=(), flops=10**9, vmem=4):
    space = pl.BlockSpec(memory_space=pltpu.VMEM)
    return pl.pallas_call(
        kernel,
        in_specs=[space] * len(args),
        out_specs=[space] * len(outs),
        out_shape=[jax.ShapeDtypeStruct(shape, dtype) for shape, dtype in outs],
        scratch_shapes=[pltpu.VMEM(shape, dtype) for shape, dtype in scratch],
        cost_estimate=pl.CostEstimate(flops=flops, bytes_accessed=4 * 10**6, transcendentals=0),
        compiler_params=pltpu.CompilerParams(vmem_limit_bytes=vmem << 20),
    )(*args)


def relay_weight(half, bit):
    near = swap_col(half)
    far = swap(near, DP, bit)
    return near, far, swap_row(near), swap_row(far)


def swap_mixed(values, even, odd):
    dp, row, col = (lax.axis_size(name) for name in (DP, ROW, COL))
    pairs = []
    for i in range(dp * row * col):
        c, r, d = i % col, i // col % row, i // (col * row)
        bit = odd if r else even
        if bit is None:
            c = c ^ 1
        else:
            d = d ^ (1 << bit)
        pairs.append((i, (d * row + r) * col + c))
    return lax.ppermute(values, (DP, ROW, COL), pairs)


def mixed_put(side_ref, sum_of, own_ref, away_ref):
    half = own_ref.shape[0] // 2
    r, s = side_ref[ROW_FLAG, 0], side_ref[0, 0]

    def put(ref, at, c, x):
        rows = pl.ds(pl.multiple_of(x * half, 16), half)
        ref[at * half : (at + 1) * half] = sum_of(c, rows)

    put(own_ref, 0, 0, r * s)
    put(own_ref, 1, r, 1 - r * (1 - s))
    put(away_ref, 0, 1 - r, r * (1 - s))
    put(away_ref, 1, 1, 1 - r * s)


def mixed_first_kernel(side_ref, keep_ref, got_ref, own_ref, away_ref):
    mixed_put(
        side_ref, lambda c, rows: keep_ref[c, rows] + got_ref[c, rows], own_ref, away_ref
    )


def mixed_second_kernel(side_ref, own_ref, got_ref, mine_ref, away_ref):
    half = mine_ref.shape[0]
    at = (1 - side_ref[ROW_FLAG, 0]) * side_ref[0, 0]
    for ref, where in ((mine_ref, at), (away_ref, 1 - at)):
        rows = pl.ds(pl.multiple_of(where * half, 16), half)
        ref[...] = own_ref[rows] + got_ref[rows]


def reduce_weight(send, keep, sides, z_first, last, outs):
    bits = lax.axis_size(DP).bit_length() - 1
    light = 10**8
    own, got = keep, swap_row(send)
    rows = keep.shape[1]
    if z_first:
        rows //= 2
        own, away = call(
            functools.partial(halve_both_kernel, 1),
            (sides, own, got),
            [((2, rows, HALF), bf16)] * 2,
            flops=light,
        )
        got = swap(away, DP, 1)
    own, away = call(mixed_first_kernel, (sides, own, got), [((rows, HALF), bf16)] * 2, flops=light)
    got = swap_mixed(away, None, 0)
    own, away = call(
        mixed_second_kernel, (sides, own, got), [((rows // 2, HALF), bf16)] * 2, flops=light
    )
    got = swap_mixed(away, 0, None)
    for bit in range(2 if z_first else 1, bits - 1):
        own, away = call(
            functools.partial(halve_kernel, bit),
            (sides, own, got),
            [((own.shape[0] // 2, HALF), bf16)] * 2,
            flops=light,
        )
        got = swap(away, DP, bit)
    (own,) = call(add_kernel, (own, got), [(own.shape, bf16)], flops=light)
    got = swap(own, DP, bits - 1)
    (own,) = call(add_kernel, (own, got), [(own.shape, bf16)], flops=light)
    for bit in reversed(range(2, bits - 1)):
        got = swap(own, DP, bit)
        (own,) = call(
            functools.partial(double_kernel, bit),
            (sides, own, got),
            [((2 * own.shape[0], HALF), bf16)],
            flops=light,
        )
    got = swap_mixed(own, 1, 0)
    (own,) = call(join_kernel, (own, got), [((2, *own.shape), bf16)], flops=light)
    got = swap_mixed(own, 0, 1)
    return call(functools.partial(last, z_first), (sides, own, got), outs, flops=light)


def shards(
    tokens,
    qkv_weight,
    qkv_bias,
    pos_table,
    rel_index,
    region_ids,
    shifts,
    proj_weight,
    proj_bias,
    layer_norm_scales,
    layer_norm_biases,
    fc1_weight,
    fc1_bias,
    fc2_weight,
    fc2_bias,
    cotangent,
):
    col, row = lax.axis_index(COL), lax.axis_index(ROW)
    me = lax.axis_index(DP)
    bits = lax.axis_size(DP).bit_length() - 1
    rows = tokens.shape[0] // 2
    down_bit = 1 if bits > 1 else 0

    def halved(weight, dim, bit):
        size = weight.shape[dim] // 2
        return lax.dynamic_slice_in_dim(weight, ((me >> bit) & 1) * size, size, dim)

    def exchange(values):
        send = lax.dynamic_slice_in_dim(values, (1 - col) * rows, rows, 0)
        return values, swap_col(send)

    qkv_block = qkv_weight.transpose(1, 0, 2)
    qkv_far = relay_weight(halved(qkv_block, 1, 0), 0)
    up_far = relay_weight(halved(fc1_weight, 1, 0), 0)
    wqkv = (qkv_block, swap_row(qkv_block), *qkv_far)
    up_row, down_row = swap_row(fc1_weight), swap_row(fc2_weight)
    proj_col = swap_col(proj_weight)
    wproj = (proj_weight, swap_row(proj_weight), proj_col, swap_row(proj_col))

    vectors = jnp.stack(
        [
            layer_norm_scales[0],
            layer_norm_scales[1],
            layer_norm_biases[0],
            layer_norm_biases[1],
            proj_bias,
            fc2_bias,
        ]
    )
    vectors = jnp.concatenate([vectors, swap_col(vectors)], axis=1)
    bias_qkv = jnp.concatenate([qkv_bias, swap_row(qkv_bias)], axis=1)
    bias_row = swap_row(fc1_bias)
    table = pos_table.T
    table = jnp.concatenate([table, swap_row(table)], axis=0)
    heads, entries = table.shape
    flags = [(me >> bit) & 1 for bit in range(min(bits, ROW_FLAG))]
    flags += [jnp.int32(0)] * (ROW_FLAG - len(flags)) + [row, col, shifts[0], shifts[1]]
    sides_in = jnp.broadcast_to(jnp.stack(flags).astype(jnp.int32)[:, None], (len(flags), 128))

    index_t = rel_index.T
    lookup = (index_t.reshape(-1)[:, None] == jnp.arange(entries)[None, :]).astype(f32)
    pos = lax.dot_general(table, lookup, (((1,), (1,)), ((), ())), precision=highest)
    pos = pos.reshape(heads, CELLS, CELLS)
    per_side = SIDE // WIN
    zones = region_ids.reshape(per_side, WIN, per_side, WIN).transpose(0, 2, 1, 3)
    zones = zones.reshape(per_side * per_side, CELLS)
    down_half = halved(fc2_weight, 0, down_bit)
    down_far = relay_weight(down_half, down_bit)
    allowed = zones[:, :, None] == zones[:, None, :]
    biased = jnp.where(allowed[:, None], pos[None], masked_value)

    def corner(values, low, fill):
        high = PAIR - low - CELLS
        pad = [(0, 0)] * (values.ndim - 2) + [(low, high), (low, high + 128 - PAIR)]
        return jnp.pad(values, pad, constant_values=fill)

    bias = jnp.maximum(
        corner(biased[0::2], 0, masked_value), corner(biased[1::2], CELLS, masked_value)
    )
    pair_index = jnp.maximum(corner(index_t, 0, -1), corner(index_t, CELLS, -1))

    x_own, x_other = exchange(tokens)
    z_own, z_other = exchange(cotangent)

    count = rows // IMAGE * 2 * PAIR
    width = 2 * tokens.shape[1]
    wide = (count, width)
    x, a1, order, sides = call(
        enter_kernel,
        (sides_in, x_own, x_other, vectors),
        [(wide, bf16), (wide, bf16), ((2 * PAIR, IMAGE), bf16), (sides_in.shape, jnp.int32)],
    )
    q, k, v = call(qkv_kernel, (sides, a1, *wqkv, bias_qkv), [(wide, bf16)] * 3)
    probs, o = call(
        attend_kernel,
        (q, k, v, bias),
        [((count // PAIR, heads, PAIR, 128), bf16), (wide, bf16)],
        vmem=8,
    )
    h1, a2 = call(proj_kernel, (x, o, *wproj, vectors), [(wide, f32), (wide, bf16)])
    (dz,) = call(arrange_kernel, (sides, z_own, z_other, order), [(wide, bf16)])
    hidden = fc1_weight.shape[1]
    block = ((2, hidden, HALF), bf16)
    acc, da2, send2, send1, other_sum, a2_t = call(
        functools.partial(mlp_kernel, 1, down_bit),
        (sides, a2, dz, bias_row[None], vectors, up_row, *up_far[2:], down_row, *down_far[2:], h1),
        [(wide, f32), (wide, f32), block, block, ((1, hidden), f32), (wide[::-1], bf16)],
        flops=10**9,
        vmem=8,
    )
    out_rows, da2, keep2, keep1, mine_sum = call(
        functools.partial(mlp_kernel, 0, down_bit),
        (
            sides,
            a2,
            dz,
            fc1_bias[None],
            vectors,
            fc1_weight,
            *up_far[:2],
            fc2_weight,
            *down_far[:2],
            acc,
            da2,
            a2_t,
        ),
        [(wide, bf16), (wide, f32), block, block, ((1, hidden), f32)],
        scratch=[(wide, f32)],
        flops=10**9,
        vmem=8,
    )
    (fc2_grad,) = reduce_weight(send2, keep2, sides, False, last_fc2_kernel, [(fc2_weight.shape, f32)])
    (fc1_grad,) = reduce_weight(send1, keep1, sides, True, last_fc1_kernel, [(fc1_weight.shape, f32)])

    blockp = ((2, *proj_weight.shape), bf16)
    dh1, do, sendp, keepp, sums_two = call(
        mid_kernel,
        (da2, h1, dz, o, *wproj, vectors),
        [(wide, f32), (wide, bf16), blockp, blockp, ((4, width), f32)],
        scratch=[(wide, bf16)],
    )
    dq, dk, dv, ds = call(
        attend_back_kernel,
        (q, k, v, probs, do),
        [(wide, bf16)] * 3 + [((heads, PAIR, 128), f32)],
        vmem=8,
    )
    sendq, keepq, sums_qkv = call(
        qkv_grad_kernel, (a1, dq, dk, dv, sendp, keepp), [block, block, ((2, width), f32)]
    )
    half = ((2, rows, tokens.shape[1]), bf16)
    own_rows, other_rows, sums_one = call(
        leave_kernel,
        (sides, dq, dk, dv, dh1, x, *wqkv, vectors, order, out_rows),
        [half, half, ((2, width), f32)],
        scratch=[(wide, bf16)],
    )
    out, grad_input = call(
        finish_kernel,
        (sides, own_rows, swap_col(other_rows)),
        [(tokens.shape, bf16), (tokens.shape, f32)],
    )
    (table_sums,) = call(table_kernel, (ds, pair_index), [((heads, HALF), f32)])
    qkv_grad, proj_grad = reduce_weight(
        sendq,
        keepq,
        sides,
        False,
        last_qkv_kernel,
        [((3, HALF, HALF), f32), (proj_weight.shape, f32)],
    )
    sent, own = call(
        pack_kernel,
        (sums_qkv, mine_sum, other_sum, table_sums, sums_one, sums_two),
        [((32, HALF), f32)] * 2,
    )
    small = ((24, HALF), f32)
    own, away = call(split_kernel, (own, swap_row(sent)), [small] * 2)
    got = swap_col(away)
    for bit in range(bits):
        (own,) = call(add_kernel, (own, got), [small])
        got = swap(own, DP, bit)
    two = ((2, HALF), f32)
    one = ((1, HALF), f32)
    (
        qkv_bias_grad,
        fc1_bias_grad,
        table_grad,
        gains_grad,
        shifts_grad,
        proj_bias_grad,
        fc2_bias_grad,
    ) = call(
        unpack_kernel,
        (own, got),
        [two, ((1, hidden), f32), ((heads // 2, entries), f32), two, two, one, one],
    )
    return (
        out,
        grad_input,
        qkv_grad.transpose(1, 0, 2),
        qkv_bias_grad,
        table_grad.T,
        proj_grad,
        proj_bias_grad[0],
        gains_grad,
        shifts_grad,
        fc1_grad,
        fc1_bias_grad[0],
        fc2_grad,
        fc2_bias_grad[0],
    )


def solution(mesh):
    return jax.shard_map(
        shards,
        mesh=mesh,
        in_specs=(
            P((DP, ROW), COL),
            P(COL, None, ROW),
            P(None, ROW),
            P(None, ROW),
            P(),
            P(),
            P(),
            P(ROW, COL),
            P(COL),
            P(None, COL),
            P(None, COL),
            P(COL, ROW),
            P(ROW),
            P(ROW, COL),
            P(COL),
            P((DP, ROW), COL),
        ),
        out_specs=(
            P((DP, ROW), COL),
            P((DP, ROW), COL),
            P(COL, None, ROW),
            P(None, ROW),
            P(None, ROW),
            P(ROW, COL),
            P(COL),
            P(None, COL),
            P(None, COL),
            P(COL, ROW),
            P(ROW),
            P(ROW, COL),
            P(COL),
        ),
        check_vma=False,
    )
```

```python
import functools

import jax
import jax.numpy as jnp
from jax import lax
from jax.experimental import pallas as pl
from jax.experimental.pallas import tpu as pltpu
from jax.sharding import PartitionSpec as P


HEAD_DIM = 32
WIN = 7
SIDE = 14
CELLS = WIN * WIN
IMAGE = SIDE * SIDE
PAIR = 112
GROUP = 128 // HEAD_DIM

highest = lax.Precision.HIGHEST
epsilon = 1e-05
masked_value = -1000000000.0
score_scale = HEAD_DIM ** (-0.5)
f32 = jnp.float32
bf16 = jnp.bfloat16


DP, ROW, COL = "dp", "row", "col"


def swap(values, axis, bit=0):
    size = lax.axis_size(axis)
    return lax.ppermute(values, axis, [(i, i ^ (1 << bit)) for i in range(size)])


def swap_row(values):
    return swap(values, ROW)


def swap_col(values):
    return swap(values, COL)


def dot(a, b):
    return jnp.dot(a, b, preferred_element_type=f32)


def dot_nt(a, b):
    return lax.dot_general(a, b, (((1,), (1,)), ((), ())), preferred_element_type=f32)


def dot_tn(a, b):
    return lax.dot_general(a, b, (((0,), (0,)), ((), ())), preferred_element_type=f32)


def lane_group():
    return lax.broadcasted_iota(jnp.int32, (PAIR, 128), 1) // HEAD_DIM


def fill_lanes(rows):
    return jnp.concatenate([rows, jnp.zeros((128 - PAIR, 128), rows.dtype)], axis=0)


def stack_heads(rows, lanes):
    zero = jnp.zeros_like(rows)
    return jnp.concatenate([jnp.where(lanes == j, rows, zero) for j in range(GROUP)], axis=0)


def pick_heads(parts, lanes):
    total = parts[0]
    for j in range(1, GROUP):
        total = jnp.where(lanes == j, parts[j], total)
    return total


def attend_kernel(q_ref, k_ref, v_ref, bias_ref, p_ref, o_ref):
    lanes = lane_group()

    @pl.loop(0, q_ref.shape[0] // PAIR)
    def _(i):
        rows = pl.ds(pl.multiple_of(i * PAIR, PAIR), PAIR)
        for g in range(bias_ref.shape[1] // GROUP):
            cols = slice(g * 128, (g + 1) * 128)
            heads = slice(g * GROUP, (g + 1) * GROUP)
            v = v_ref[rows, cols]
            s = dot_nt(stack_heads(k_ref[rows, cols], lanes), fill_lanes(q_ref[rows, cols]))
            s = s.reshape(GROUP, PAIR, 128) * score_scale + bias_ref[lax.rem(i, 2), heads]
            e = jnp.exp(s - jnp.max(s, axis=1, keepdims=True))
            p = (e * (1.0 / jnp.sum(e, axis=1, keepdims=True))).astype(bf16)
            p_ref[i, heads] = p
            o_ref[rows, cols] = pick_heads(
                [dot_tn(p[j], v)[:PAIR] for j in range(GROUP)], lanes
            ).astype(bf16)


def attend_back_kernel(q_ref, k_ref, v_ref, p_ref, do_ref, dq_ref, dk_ref, dv_ref, ds_ref):
    lanes = lane_group()
    ds_ref[...] = jnp.zeros_like(ds_ref)

    @pl.loop(0, q_ref.shape[0] // PAIR, unroll=True)
    def _(i):
        rows = pl.ds(pl.multiple_of(i * PAIR, PAIR), PAIR)
        for g in range(p_ref.shape[1] // GROUP):
            cols = slice(g * 128, (g + 1) * 128)
            heads = slice(g * GROUP, (g + 1) * GROUP)
            k = k_ref[rows, cols]
            q = fill_lanes(q_ref[rows, cols])
            do = fill_lanes(do_ref[rows, cols])
            p = p_ref[i, heads]
            pf = p.astype(f32)
            dp = dot_nt(stack_heads(v_ref[rows, cols], lanes), do).reshape(GROUP, PAIR, 128)
            ds = (pf * (dp - jnp.sum(pf * dp, axis=1, keepdims=True))).astype(bf16)
            ds_ref[heads] += ds.astype(f32)
            dk = dot(ds.reshape(GROUP * PAIR, 128), q).reshape(GROUP, PAIR, 128)
            dv = dot(p.reshape(GROUP * PAIR, 128), do).reshape(GROUP, PAIR, 128)
            dq = [dot_tn(ds[j], k)[:PAIR] for j in range(GROUP)]
            dq_ref[rows, cols] = (pick_heads(dq, lanes) * score_scale).astype(bf16)
            dk_ref[rows, cols] = (pick_heads(dk, lanes) * score_scale).astype(bf16)
            dv_ref[rows, cols] = pick_heads(dv, lanes).astype(bf16)


def table_kernel(ds_ref, index_ref, out_ref):
    entries = lax.broadcasted_iota(jnp.int32, (HALF, 128), 0).astype(f32).astype(bf16)
    one_hit, no_hit = jnp.ones((HALF, 128), bf16), jnp.zeros((HALF, 128), bf16)
    heads = ds_ref.shape[0]
    out_ref[...] = jnp.zeros_like(out_ref)

    @pl.loop(0, WIN)
    def _(step):
        total = jnp.zeros((2 * heads, HALF), f32)
        for one in range(WIN):
            k = step * WIN + one
            ds = ds_ref[:, pl.ds(k, 1), :].reshape(heads, 128)
            second = ds_ref[:, pl.ds(k + CELLS, 1), :].reshape(heads, 128)
            ds = ds + jnp.concatenate([second[:, CELLS:], second[:, :CELLS]], axis=1)
            high = ds.astype(bf16)
            low = (ds - high.astype(f32)).astype(bf16)
            hit = jnp.where(entries == index_ref[pl.ds(k, 1), :].astype(bf16), one_hit, no_hit)
            total = total + dot_nt(jnp.concatenate([high, low], axis=0), hit)
        out_ref[...] += total[:heads] + total[heads:]


def chunked(rows, body):
    @pl.loop(0, rows // PAIR, unroll=True)
    def _(i):
        body(pl.ds(pl.multiple_of(i * PAIR, PAIR), PAIR))


def standardize(values):
    center = jnp.mean(values, axis=1, keepdims=True)
    centered = values - center
    scaling = lax.rsqrt(jnp.mean(centered * centered, axis=1, keepdims=True) + epsilon)
    return centered * scaling, scaling


def standardize_back(grad, hat, scaling, gain):
    scaled = grad * gain
    first = jnp.mean(scaled, axis=1, keepdims=True)
    second = jnp.mean(scaled * hat, axis=1, keepdims=True)
    return scaling * (scaled - first - hat * second)


def add_sum(ref, row, values):
    ref[row : row + 1, :] += jnp.sum(values, axis=0, keepdims=True)


ROW_FLAG, COL_FLAG, SHIFT_FLAG = 4, 5, 6
GAIN1, GAIN2, SHIFT1, SHIFT2, BIAS_PROJ, BIAS_FC2 = range(6)
HALF = 256


def window_order(shift_i, shift_j):
    place = lax.broadcasted_iota(jnp.int32, (2 * PAIR, 1), 0)
    pair = (place >= PAIR).astype(jnp.int32)
    inside = place - PAIR * pair
    right = (inside >= CELLS).astype(jnp.int32)
    spot = inside - CELLS * right
    down = (spot * 37) >> 8
    i = pair * WIN + down + shift_i
    j = right * WIN + spot - WIN * down + shift_j
    i = jnp.where(i >= SIDE, i - SIDE, i)
    j = jnp.where(j >= SIDE, j - SIDE, j)
    token = jnp.where(inside < 2 * CELLS, i * SIDE + j, -1)
    hit = token == lax.broadcasted_iota(jnp.int32, (2 * PAIR, IMAGE), 1)
    return hit.astype(f32).astype(bf16)


def my_half(ref, at):
    rows = ref.shape[0] // 2
    return ref[pl.ds(pl.multiple_of(at * rows, 8), rows)]


def enter_kernel(side_in, own_ref, other_ref, vec_ref, x_ref, a_ref, order_ref, side_ref):
    side_ref[...] = side_in[...]
    order_ref[...] = window_order(side_in[SHIFT_FLAG, 0], side_in[SHIFT_FLAG + 1, 0])
    images = other_ref.shape[0] // IMAGE
    own = my_half(own_ref, side_in[COL_FLAG, 0])
    for n in range(images):
        rows = slice(n * IMAGE, (n + 1) * IMAGE)
        tok = jnp.concatenate([own[rows], other_ref[rows]], axis=1)
        x = dot(order_ref[...], tok)
        hat, _ = standardize(x)
        a = hat * vec_ref[GAIN1 : GAIN1 + 1] + vec_ref[SHIFT1 : SHIFT1 + 1]
        out = slice(n * 2 * PAIR, (n + 1) * 2 * PAIR)
        x_ref[out] = x.astype(bf16)
        a_ref[out] = a.astype(bf16)


def qkv_kernel(side_ref, a_ref, w0, w1, n2, f2, n3, f3, bias_ref, q_ref, k_ref, v_ref):
    s = side_ref[0, 0]
    near = a_ref[:, pl.ds(pl.multiple_of(HALF + s * 128, 128), 128)]
    far = a_ref[:, pl.ds(pl.multiple_of(HALF + (1 - s) * 128, 128), 128)]
    for side, (top, low0, low1) in enumerate(((w0, n2, f2), (w1, n3, f3))):
        cols = slice(side * HALF, (side + 1) * HALF)
        for j, ref in enumerate((q_ref, k_ref, v_ref)):
            y = dot(a_ref[:, :HALF], top[j]) + dot(near, low0[j]) + dot(far, low1[j])
            if j != 1:
                y = y + bias_ref[j // 2 : j // 2 + 1, cols]
            ref[:, cols] = y.astype(bf16)


def proj_kernel(x_ref, o_ref, w0, w1, w2, w3, vec_ref, h_ref, a_ref):
    o0, o1 = o_ref[:, :HALF], o_ref[:, HALF:]
    h_ref[:, :HALF] = dot(o0, w0[...]) + dot(o1, w1[...])
    h_ref[:, HALF:] = dot(o0, w2[...]) + dot(o1, w3[...])

    def body(rows):
        h = x_ref[rows].astype(f32) + h_ref[rows] + vec_ref[BIAS_PROJ : BIAS_PROJ + 1]
        hat, _ = standardize(h)
        h_ref[rows] = h
        a_ref[rows] = (
            hat * vec_ref[GAIN2 : GAIN2 + 1] + vec_ref[SHIFT2 : SHIFT2 + 1]
        ).astype(bf16)

    chunked(x_ref.shape[0], body)


def mlp_kernel(side, down_bit, *refs):
    side_ref, a_ref, dz_ref, bias_ref, vec_ref = refs[:5]
    u, w = refs[5:8], refs[8:11]
    if side:
        h_ref = refs[11]
        acc_ref, da_ref, grad2_ref, grad1_ref, bsum_ref, at_ref = refs[12:]
        at_ref[...] = a_ref[...].T
        acc_ref[...] = h_ref[...] + vec_ref[BIAS_FC2 : BIAS_FC2 + 1]
        da_ref[...] = jnp.zeros_like(da_ref)
        acc_in, da_in = acc_ref, da_ref
    else:
        acc_in, da_in, at_ref = refs[11:14]
        out_ref, da_ref, grad2_ref, grad1_ref, bsum_ref, acc_ref = refs[14:]
        acc_ref[...] = acc_in[...]
        da_ref[...] = da_in[...]
    hidden = u[0].shape[1]
    width = hidden // 2
    same = side_ref[0, 0] == side_ref[down_bit, 0]

    for half in range(2):
        up, down, down_else = u[1 + half], w[1 + half], w[2 - half]
        first = side_ref[0, 0] if half == 0 else 1 - side_ref[0, 0]
        tile = pl.ds(pl.multiple_of(first * width, width), width)
        p = jnp.concatenate([u[0][:, tile], up[...]], axis=0)
        d = jnp.concatenate([w[0][tile], jnp.where(same, down[...], down_else[...])], axis=1)
        z = dz_ref[...]
        f = dot(a_ref[...], p) + bias_ref[:, tile]
        dm = dot_nt(z, d)
        cdf = 0.5 * (1.0 + lax.erf(f * (0.5**0.5)))
        m = (f * cdf).astype(bf16)
        slope = cdf + f * (jnp.exp(-0.5 * f * f) * 0.3989422804014327)
        df = (dm * slope).astype(bf16)
        bsum_ref[:, tile] = jnp.sum(df.astype(f32), axis=0, keepdims=True)
        acc_ref[...] += dot(m, d)
        da_ref[...] += dot_nt(df, p)
        g2 = dot(m.T, z).astype(bf16)
        grad2_ref[0, tile], grad2_ref[1, tile] = g2[:, :HALF], g2[:, HALF:]
        g1 = dot(at_ref[...], df).astype(bf16)
        for t in range(width // HALF):
            rows = pl.ds(pl.multiple_of(first * width + t * HALF, HALF), HALF)
            for c in range(2):
                grad1_ref[c, rows] = g1[c * HALF : (c + 1) * HALF, t * HALF : (t + 1) * HALF]

    if not side:
        out_ref[...] = acc_ref[...].astype(bf16)


def mid_kernel(
    da_ref, h_ref, dz_ref, o_ref, w0, w1, w2, w3, vec_ref, dh_ref, do_ref, send_ref, keep_ref, sum_ref, dy_ref
):
    sum_ref[...] = jnp.zeros_like(sum_ref)

    def body(rows):
        hat, scaling = standardize(h_ref[rows])
        da = da_ref[rows]
        dz = dz_ref[rows].astype(f32)
        du = standardize_back(da, hat, scaling, vec_ref[GAIN2 : GAIN2 + 1])
        dh = dz + du
        dh_ref[rows] = dh
        dy = dh.astype(bf16)
        dy_ref[rows] = dy
        add_sum(sum_ref, 0, da * hat)
        add_sum(sum_ref, 1, da)
        add_sum(sum_ref, 2, dy.astype(f32))
        add_sum(sum_ref, 3, dz)

    chunked(h_ref.shape[0], body)
    y0, y1 = dy_ref[:, :HALF], dy_ref[:, HALF:]
    do_ref[:, :HALF] = (dot_nt(y0, w0[...]) + dot_nt(y1, w2[...])).astype(bf16)
    do_ref[:, HALF:] = (dot_nt(y0, w1[...]) + dot_nt(y1, w3[...])).astype(bf16)
    ot = o_ref[...].T
    for side, ref in enumerate((keep_ref, send_ref)):
        for c in range(2):
            ref[c] = dot(
                ot[side * HALF : (side + 1) * HALF], dy_ref[:, c * HALF : (c + 1) * HALF]
            ).astype(bf16)


def qkv_grad_kernel(a_ref, dq_ref, dk_ref, dv_ref, sendp_ref, keepp_ref, send_ref, keep_ref, sum_ref):
    at = a_ref[...].T
    for side, (ref, proj_ref) in enumerate(((keep_ref, keepp_ref), (send_ref, sendp_ref))):
        cols = slice(side * HALF, (side + 1) * HALF)
        ref[:, 3 * HALF :] = proj_ref[...]
        for j, d_ref in enumerate((dq_ref, dk_ref, dv_ref)):
            d = d_ref[:, cols]
            for c in range(2):
                ref[c, j * HALF : (j + 1) * HALF] = dot(at[c * HALF : (c + 1) * HALF], d).astype(bf16)
            if j != 1:
                sum_ref[j // 2 : j // 2 + 1, cols] = jnp.sum(d.astype(f32), axis=0, keepdims=True)


def leave_kernel(
    side_ref,
    dq_ref,
    dk_ref,
    dv_ref,
    dh_ref,
    x_ref,
    w0,
    w1,
    n2,
    f2,
    n3,
    f3,
    vec_ref,
    order_ref,
    out_ref,
    own_ref,
    other_ref,
    sum_ref,
    g_ref,
    da_ref,
    all_ref,
):
    sum_ref[...] = jnp.zeros_like(sum_ref)

    def part(mine, other):
        total = None
        for j, ref in enumerate((dq_ref, dk_ref, dv_ref)):
            y = dot_nt(ref[:, :HALF], mine(j)) + dot_nt(ref[:, HALF:], other(j))
            total = y if total is None else total + y
        return total

    near = pl.ds(pl.multiple_of(side_ref[0, 0] * 128, 128), 128)
    far = pl.ds(pl.multiple_of((1 - side_ref[0, 0]) * 128, 128), 128)
    for j in range(3):
        for side, (ref_n, ref_f) in enumerate(((n2, f2), (n3, f3))):
            all_ref[side, j, near] = ref_n[j]
            all_ref[side, j, far] = ref_f[j]
    da_ref[:, :HALF] = part(lambda j: w0[j], lambda j: w1[j])
    da_ref[:, HALF:] = part(lambda j: all_ref[0, j], lambda j: all_ref[1, j])

    def body(rows):
        da = da_ref[rows]
        hat, scaling = standardize(x_ref[rows].astype(f32))
        du = standardize_back(da, hat, scaling, vec_ref[GAIN1 : GAIN1 + 1])
        g_ref[rows] = (dh_ref[rows] + du).astype(bf16)
        add_sum(sum_ref, 0, da * hat)
        add_sum(sum_ref, 1, da)

    chunked(x_ref.shape[0], body)
    for j, rows_ref in enumerate((out_ref, g_ref)):
        for n in range(own_ref.shape[1] // IMAGE):
            g = dot_tn(order_ref[...], rows_ref[n * 2 * PAIR : (n + 1) * 2 * PAIR])
            at = slice(n * IMAGE, (n + 1) * IMAGE)
            own_ref[j, at] = g[:, :HALF].astype(bf16)
            other_ref[j, at] = g[:, HALF:].astype(bf16)


def finish_kernel(side_ref, own_ref, got_ref, out_ref, grad_ref):
    rows = own_ref.shape[1]
    at = side_ref[COL_FLAG, 0]
    for ref, place in ((own_ref, at), (got_ref, 1 - at)):
        where = pl.ds(pl.multiple_of(place * rows, 8), rows)
        out_ref[where] = ref[0]
        grad_ref[where] = ref[1].astype(f32)


def arrange_kernel(side_ref, own_ref, other_ref, order_ref, out_ref):
    images = other_ref.shape[0] // IMAGE
    own = my_half(own_ref, side_ref[COL_FLAG, 0])
    for n in range(images):
        rows = slice(n * IMAGE, (n + 1) * IMAGE)
        tok = jnp.concatenate([own[rows], other_ref[rows]], axis=1)
        out_ref[n * 2 * PAIR : (n + 1) * 2 * PAIR] = dot(order_ref[...], tok).astype(bf16)


def halve_both_kernel(bit, side_ref, keep_ref, got_ref, mine_ref, away_ref):
    half = mine_ref.shape[1]
    for ref, at in ((mine_ref, side_ref[bit, 0]), (away_ref, 1 - side_ref[bit, 0])):
        rows = pl.ds(pl.multiple_of(at * half, 16), half)
        ref[...] = keep_ref[:, rows] + got_ref[:, rows]


def halve_kernel(bit, side_ref, own_ref, got_ref, mine_ref, away_ref):
    half = mine_ref.shape[0]
    for ref, at in ((mine_ref, side_ref[bit, 0]), (away_ref, 1 - side_ref[bit, 0])):
        rows = pl.ds(pl.multiple_of(at * half, 16), half)
        ref[...] = own_ref[rows] + got_ref[rows]


def add_kernel(own_ref, got_ref, out_ref):
    out_ref[...] = own_ref[...] + got_ref[...]


def double_kernel(bit, side_ref, own_ref, got_ref, out_ref):
    half = own_ref.shape[0]
    for ref, at in ((own_ref, side_ref[bit, 0]), (got_ref, 1 - side_ref[bit, 0])):
        out_ref[pl.ds(pl.multiple_of(at * half, 16), half)] = ref[...]


def join_kernel(own_ref, got_ref, out_ref):
    out_ref[0] = own_ref[...]
    out_ref[1] = got_ref[...]


def quarters(z_first, side_ref, own_ref, got_ref):
    r, x, z = side_ref[ROW_FLAG, 0], side_ref[0, 0], side_ref[1, 0]

    def place(x, z):
        return 2 * z + x if z_first else 2 * x + z

    mixed_x, mixed_z = x + r * (1 - 2 * x), z + (1 - r) * (1 - 2 * z)
    return (
        (own_ref[0], place(x, z)),
        (own_ref[1], place(mixed_x, mixed_z)),
        (got_ref[0], place(1 - mixed_x, 1 - mixed_z)),
        (got_ref[1], place(1 - x, 1 - z)),
    )


def last_fc2_kernel(z_first, side_ref, own_ref, got_ref, out_ref):
    rows = own_ref.shape[1]
    for values, at in quarters(z_first, side_ref, own_ref, got_ref):
        out_ref[pl.ds(pl.multiple_of(at * rows, 16), rows)] = values.astype(f32)


def last_fc1_kernel(z_first, side_ref, own_ref, got_ref, out_ref):
    for values, at in quarters(z_first, side_ref, own_ref, got_ref):
        out_ref[:, pl.ds(pl.multiple_of(at * HALF, HALF), HALF)] = values.astype(f32)


def last_qkv_kernel(z_first, side_ref, own_ref, got_ref, qkv_ref, proj_ref):
    for values, at in quarters(z_first, side_ref, own_ref, got_ref):

        @pl.when(at == 3)
        def _(values=values):
            proj_ref[...] = values.astype(f32)

        @pl.when(at < 3)
        def _(values=values, at=at):
            qkv_ref[pl.ds(lax.min(at, 2), 1)] = values.astype(f32)[None]


SPLIT, FEATURES = 14, 6


def pack_kernel(qkv_ref, mine1_ref, other1_ref, table_ref, one_ref, two_ref, send_ref, keep_ref):
    for side, (ref, fc1_ref) in enumerate(((keep_ref, mine1_ref), (send_ref, other1_ref))):
        cols = slice(side * HALF, (side + 1) * HALF)
        ref[...] = jnp.zeros_like(ref)
        ref[0:2] = qkv_ref[:, cols]
        for t in range(4):
            ref[2 + t : 3 + t] = fc1_ref[:, t * HALF : (t + 1) * HALF]
        ref[6:SPLIT] = table_ref[side * 8 : side * 8 + 8]
        for c in range(2):
            at, half = SPLIT + c * FEATURES, slice(c * HALF, (c + 1) * HALF)
            ref[at : at + 2] = one_ref[:, half]
            ref[at + 2 : at + 6] = two_ref[:, half]


def split_kernel(keep_ref, got_ref, own_ref, away_ref):
    total = keep_ref[...] + got_ref[...]
    end = SPLIT + FEATURES
    for ref, at in ((own_ref, SPLIT), (away_ref, end)):
        ref[...] = jnp.zeros_like(ref)
        ref[:SPLIT] = total[:SPLIT]
        ref[SPLIT:end] = total[at : at + FEATURES]


def unpack_kernel(own_ref, got_ref, bq_ref, b1_ref, table_ref, gain_ref, shift_ref, bp_ref, b2_ref):
    total = own_ref[...] + got_ref[...]
    bq_ref[...] = total[0:2]
    for t in range(4):
        b1_ref[:, t * HALF : (t + 1) * HALF] = total[2 + t : 3 + t]
    table_ref[...] = total[6:SPLIT, : table_ref.shape[1]]
    for j in range(2):
        gain_ref[j : j + 1] = total[SPLIT + 2 * j : SPLIT + 2 * j + 1]
        shift_ref[j : j + 1] = total[SPLIT + 2 * j + 1 : SPLIT + 2 * j + 2]
    bp_ref[...] = total[SPLIT + 4 : SPLIT + 5]
    b2_ref[...] = total[SPLIT + 5 : SPLIT + 6]


def call(kernel, args, outs, scratch=(), flops=10**9, vmem=4):
    space = pl.BlockSpec(memory_space=pltpu.VMEM)
    return pl.pallas_call(
        kernel,
        in_specs=[space] * len(args),
        out_specs=[space] * len(outs),
        out_shape=[jax.ShapeDtypeStruct(shape, dtype) for shape, dtype in outs],
        scratch_shapes=[pltpu.VMEM(shape, dtype) for shape, dtype in scratch],
        cost_estimate=pl.CostEstimate(flops=flops, bytes_accessed=4 * 10**6, transcendentals=0),
        compiler_params=pltpu.CompilerParams(vmem_limit_bytes=vmem << 20),
    )(*args)


def relay_weight(half, bit):
    near = swap_col(half)
    far = swap(near, DP, bit)
    return near, far, swap_row(near), swap_row(far)


def swap_mixed(values, even, odd):
    dp, row, col = (lax.axis_size(name) for name in (DP, ROW, COL))
    pairs = []
    for i in range(dp * row * col):
        c, r, d = i % col, i // col % row, i // (col * row)
        bit = odd if r else even
        if bit is None:
            c = c ^ 1
        else:
            d = d ^ (1 << bit)
        pairs.append((i, (d * row + r) * col + c))
    return lax.ppermute(values, (DP, ROW, COL), pairs)


def mixed_put(side_ref, sum_of, own_ref, away_ref):
    half = own_ref.shape[0] // 2
    r, s = side_ref[ROW_FLAG, 0], side_ref[0, 0]

    def put(ref, at, c, x):
        rows = pl.ds(pl.multiple_of(x * half, 16), half)
        ref[at * half : (at + 1) * half] = sum_of(c, rows)

    put(own_ref, 0, 0, r * s)
    put(own_ref, 1, r, 1 - r * (1 - s))
    put(away_ref, 0, 1 - r, r * (1 - s))
    put(away_ref, 1, 1, 1 - r * s)


def mixed_first_kernel(side_ref, keep_ref, got_ref, own_ref, away_ref):
    mixed_put(
        side_ref, lambda c, rows: keep_ref[c, rows] + got_ref[c, rows], own_ref, away_ref
    )


def mixed_second_kernel(side_ref, own_ref, got_ref, mine_ref, away_ref):
    half = mine_ref.shape[0]
    at = (1 - side_ref[ROW_FLAG, 0]) * side_ref[0, 0]
    for ref, where in ((mine_ref, at), (away_ref, 1 - at)):
        rows = pl.ds(pl.multiple_of(where * half, 16), half)
        ref[...] = own_ref[rows] + got_ref[rows]


def reduce_weight(send, keep, sides, z_first, last, outs):
    bits = lax.axis_size(DP).bit_length() - 1
    light = 10**8
    own, got = keep, swap_row(send)
    rows = keep.shape[1]
    if z_first:
        rows //= 2
        own, away = call(
            functools.partial(halve_both_kernel, 1),
            (sides, own, got),
            [((2, rows, HALF), bf16)] * 2,
            flops=light,
        )
        got = swap(away, DP, 1)
    own, away = call(mixed_first_kernel, (sides, own, got), [((rows, HALF), bf16)] * 2, flops=light)
    got = swap_mixed(away, None, 0)
    own, away = call(
        mixed_second_kernel, (sides, own, got), [((rows // 2, HALF), bf16)] * 2, flops=light
    )
    got = swap_mixed(away, 0, None)
    for bit in range(2 if z_first else 1, bits - 1):
        own, away = call(
            functools.partial(halve_kernel, bit),
            (sides, own, got),
            [((own.shape[0] // 2, HALF), bf16)] * 2,
            flops=light,
        )
        got = swap(away, DP, bit)
    (own,) = call(add_kernel, (own, got), [(own.shape, bf16)], flops=light)
    got = swap(own, DP, bits - 1)
    (own,) = call(add_kernel, (own, got), [(own.shape, bf16)], flops=light)
    for bit in reversed(range(2, bits - 1)):
        got = swap(own, DP, bit)
        (own,) = call(
            functools.partial(double_kernel, bit),
            (sides, own, got),
            [((2 * own.shape[0], HALF), bf16)],
            flops=light,
        )
    got = swap_mixed(own, 1, 0)
    (own,) = call(join_kernel, (own, got), [((2, *own.shape), bf16)], flops=light)
    got = swap_mixed(own, 0, 1)
    return call(functools.partial(last, z_first), (sides, own, got), outs, flops=light)


def shards(
    tokens,
    qkv_weight,
    qkv_bias,
    pos_table,
    rel_index,
    region_ids,
    shifts,
    proj_weight,
    proj_bias,
    layer_norm_scales,
    layer_norm_biases,
    fc1_weight,
    fc1_bias,
    fc2_weight,
    fc2_bias,
    cotangent,
):
    col, row = lax.axis_index(COL), lax.axis_index(ROW)
    me = lax.axis_index(DP)
    bits = lax.axis_size(DP).bit_length() - 1
    rows = tokens.shape[0] // 2
    down_bit = 1 if bits > 1 else 0

    def halved(weight, dim, bit):
        size = weight.shape[dim] // 2
        return lax.dynamic_slice_in_dim(weight, ((me >> bit) & 1) * size, size, dim)

    def exchange(values):
        send = lax.dynamic_slice_in_dim(values, (1 - col) * rows, rows, 0)
        return values, swap_col(send)

    qkv_block = qkv_weight.transpose(1, 0, 2)
    qkv_far = relay_weight(halved(qkv_block, 1, 0), 0)
    up_far = relay_weight(halved(fc1_weight, 1, 0), 0)
    wqkv = (qkv_block, swap_row(qkv_block), *qkv_far)
    up_row, down_row = swap_row(fc1_weight), swap_row(fc2_weight)
    proj_col = swap_col(proj_weight)
    wproj = (proj_weight, swap_row(proj_weight), proj_col, swap_row(proj_col))

    vectors = jnp.stack(
        [
            layer_norm_scales[0],
            layer_norm_scales[1],
            layer_norm_biases[0],
            layer_norm_biases[1],
            proj_bias,
            fc2_bias,
        ]
    )
    vectors = jnp.concatenate([vectors, swap_col(vectors)], axis=1)
    bias_qkv = jnp.concatenate([qkv_bias, swap_row(qkv_bias)], axis=1)
    bias_row = swap_row(fc1_bias)
    table = pos_table.T
    table = jnp.concatenate([table, swap_row(table)], axis=0)
    heads, entries = table.shape
    flags = [(me >> bit) & 1 for bit in range(min(bits, ROW_FLAG))]
    flags += [jnp.int32(0)] * (ROW_FLAG - len(flags)) + [row, col, shifts[0], shifts[1]]
    sides_in = jnp.broadcast_to(jnp.stack(flags).astype(jnp.int32)[:, None], (len(flags), 128))

    index_t = rel_index.T
    lookup = (index_t.reshape(-1)[:, None] == jnp.arange(entries)[None, :]).astype(f32)
    pos = lax.dot_general(table, lookup, (((1,), (1,)), ((), ())), precision=highest)
    pos = pos.reshape(heads, CELLS, CELLS)
    per_side = SIDE // WIN
    zones = region_ids.reshape(per_side, WIN, per_side, WIN).transpose(0, 2, 1, 3)
    zones = zones.reshape(per_side * per_side, CELLS)
    down_half = halved(fc2_weight, 0, down_bit)
    down_far = relay_weight(down_half, down_bit)
    allowed = zones[:, :, None] == zones[:, None, :]
    biased = jnp.where(allowed[:, None], pos[None], masked_value)

    def corner(values, low, fill):
        high = PAIR - low - CELLS
        pad = [(0, 0)] * (values.ndim - 2) + [(low, high), (low, high + 128 - PAIR)]
        return jnp.pad(values, pad, constant_values=fill)

    bias = jnp.maximum(
        corner(biased[0::2], 0, masked_value), corner(biased[1::2], CELLS, masked_value)
    )
    pair_index = corner(index_t, 0, -1)

    x_own, x_other = exchange(tokens)
    z_own, z_other = exchange(cotangent)

    count = rows // IMAGE * 2 * PAIR
    width = 2 * tokens.shape[1]
    wide = (count, width)
    x, a1, order, sides = call(
        enter_kernel,
        (sides_in, x_own, x_other, vectors),
        [(wide, bf16), (wide, bf16), ((2 * PAIR, IMAGE), bf16), (sides_in.shape, jnp.int32)],
    )
    q, k, v = call(qkv_kernel, (sides, a1, *wqkv, bias_qkv), [(wide, bf16)] * 3)
    probs, o = call(
        attend_kernel,
        (q, k, v, bias),
        [((count // PAIR, heads, PAIR, 128), bf16), (wide, bf16)],
        vmem=8,
    )
    h1, a2 = call(proj_kernel, (x, o, *wproj, vectors), [(wide, f32), (wide, bf16)])
    (dz,) = call(arrange_kernel, (sides, z_own, z_other, order), [(wide, bf16)])
    hidden = fc1_weight.shape[1]
    block = ((2, hidden, HALF), bf16)
    acc, da2, send2, send1, other_sum, a2_t = call(
        functools.partial(mlp_kernel, 1, down_bit),
        (sides, a2, dz, bias_row[None], vectors, up_row, *up_far[2:], down_row, *down_far[2:], h1),
        [(wide, f32), (wide, f32), block, block, ((1, hidden), f32), (wide[::-1], bf16)],
        flops=10**9,
        vmem=8,
    )
    out_rows, da2, keep2, keep1, mine_sum = call(
        functools.partial(mlp_kernel, 0, down_bit),
        (
            sides,
            a2,
            dz,
            fc1_bias[None],
            vectors,
            fc1_weight,
            *up_far[:2],
            fc2_weight,
            *down_far[:2],
            acc,
            da2,
            a2_t,
        ),
        [(wide, bf16), (wide, f32), block, block, ((1, hidden), f32)],
        scratch=[(wide, f32)],
        flops=10**9,
        vmem=8,
    )
    (fc2_grad,) = reduce_weight(send2, keep2, sides, False, last_fc2_kernel, [(fc2_weight.shape, f32)])
    (fc1_grad,) = reduce_weight(send1, keep1, sides, True, last_fc1_kernel, [(fc1_weight.shape, f32)])

    blockp = ((2, *proj_weight.shape), bf16)
    dh1, do, sendp, keepp, sums_two = call(
        mid_kernel,
        (da2, h1, dz, o, *wproj, vectors),
        [(wide, f32), (wide, bf16), blockp, blockp, ((4, width), f32)],
        scratch=[(wide, bf16)],
    )
    dq, dk, dv, ds = call(
        attend_back_kernel,
        (q, k, v, probs, do),
        [(wide, bf16)] * 3 + [((heads, PAIR, 128), f32)],
        vmem=8,
    )
    sendq, keepq, sums_qkv = call(
        qkv_grad_kernel, (a1, dq, dk, dv, sendp, keepp), [block, block, ((2, width), f32)]
    )
    half = ((2, rows, tokens.shape[1]), bf16)
    own_rows, other_rows, sums_one = call(
        leave_kernel,
        (sides, dq, dk, dv, dh1, x, *wqkv, vectors, order, out_rows),
        [half, half, ((2, width), f32)],
        scratch=[(wide, bf16), (wide, f32), ((2, 3, HALF, HALF), bf16)],
    )
    out, grad_input = call(
        finish_kernel,
        (sides, own_rows, swap_col(other_rows)),
        [(tokens.shape, bf16), (tokens.shape, f32)],
    )
    (table_sums,) = call(table_kernel, (ds, pair_index), [((heads, HALF), f32)])
    qkv_grad, proj_grad = reduce_weight(
        sendq,
        keepq,
        sides,
        False,
        last_qkv_kernel,
        [((3, HALF, HALF), f32), (proj_weight.shape, f32)],
    )
    sent, own = call(
        pack_kernel,
        (sums_qkv, mine_sum, other_sum, table_sums, sums_one, sums_two),
        [((32, HALF), f32)] * 2,
    )
    small = ((24, HALF), f32)
    own, away = call(split_kernel, (own, swap_row(sent)), [small] * 2)
    got = swap_col(away)
    for bit in range(bits):
        (own,) = call(add_kernel, (own, got), [small])
        got = swap(own, DP, bit)
    two = ((2, HALF), f32)
    one = ((1, HALF), f32)
    (
        qkv_bias_grad,
        fc1_bias_grad,
        table_grad,
        gains_grad,
        shifts_grad,
        proj_bias_grad,
        fc2_bias_grad,
    ) = call(
        unpack_kernel,
        (own, got),
        [two, ((1, hidden), f32), ((heads // 2, entries), f32), two, two, one, one],
    )
    return (
        out,
        grad_input,
        qkv_grad.transpose(1, 0, 2),
        qkv_bias_grad,
        table_grad.T,
        proj_grad,
        proj_bias_grad[0],
        gains_grad,
        shifts_grad,
        fc1_grad,
        fc1_bias_grad[0],
        fc2_grad,
        fc2_bias_grad[0],
    )


def solution(mesh):
    return jax.shard_map(
        shards,
        mesh=mesh,
        in_specs=(
            P((DP, ROW), COL),
            P(COL, None, ROW),
            P(None, ROW),
            P(None, ROW),
            P(),
            P(),
            P(),
            P(ROW, COL),
            P(COL),
            P(None, COL),
            P(None, COL),
            P(COL, ROW),
            P(ROW),
            P(ROW, COL),
            P(COL),
            P((DP, ROW), COL),
        ),
        out_specs=(
            P((DP, ROW), COL),
            P((DP, ROW), COL),
            P(COL, None, ROW),
            P(None, ROW),
            P(None, ROW),
            P(ROW, COL),
            P(COL),
            P(None, COL),
            P(None, COL),
            P(COL, ROW),
            P(ROW),
            P(ROW, COL),
            P(COL),
        ),
        check_vma=False,
    )
```
